256 devices in a mesh: unit: 16 (over x, z_lo), day: 16 (over y, z_hi, core).
Axes of the slice: x: 4, y: 4, z: 8 (z_hi: 2, z_lo: 4; z = z_hi * 4 + z_lo), core: 2. Of those that a mesh axis runs over, the one named last changes fastest.
Arguments:
- outcomes: float32 [65536, 4096], P('unit', 'day'), may hold values from -6 to 6
- cohort: int32 [65536], P('unit'), may hold values from 0 to 8
- pre_end: int32 [8], replicated, may hold values from 1024 to 2047
- post_start: int32 [8], replicated, may hold values from 2048 to 3071
- unit_logit: float32 [8, 65536], P(None, 'unit'), may hold values from -4 to 4
- time_logit: float32 [8, 4096], P(None, 'day'), may hold values from -4 to 4
Outputs:
- unit_weights: float32 [8, 65536], P(None, 'unit')
- time_weights: float32 [8, 4096], P(None, 'day')
The draws below stay inside these ranges and needn't reach their ends.
All inputs are finite; a program needn't handle non-finite values.
Results may differ from the reference program's by a relative error of at most 0.0003.
Values sent between devices are 32-bit elements; how exact they have to be, the bound alone decides.
A program may use at most 64 MiB of HBM per device.

```python
import jax
import jax.numpy as jnp
from jax import lax

COHORTS = 8
UNITS = 65536
DAYS = 4096


def draw_outcomes(key, part):
    value_key = jax.random.fold_in(key, 11)
    values = jax.random.normal(value_key, (UNITS, DAYS), jnp.float32)
    return jnp.clip(values, -6.0, 6.0).astype(jnp.float32)


def place_ends(result, own_key, low, largest):
    index_at = [jax.random.randint(jax.random.fold_in(own_key, axis), (), 0, length) for axis, length in enumerate(result.shape)]
    longest = result.shape.index(max(result.shape))
    beside = index_at[:longest] + [(index_at[longest] + 1) % result.shape[longest]] + index_at[longest + 1:]
    return result.at[tuple(index_at)].set(low).at[tuple(beside)].set(largest)


def levels(key, shape, cuts, low, top_value):
    factor_of, own = 1.0, jax.random.fold_in(key, 6)
    for dim, shards_of in cuts:
        draws = jnp.exp(jax.random.uniform(jax.random.fold_in(own, dim), (shards_of,), jnp.float32, low / len(cuts), top_value / len(cuts)))
        factor_of = factor_of * jnp.repeat(draws, shape[dim] // shards_of).reshape([-1 if axis == dim else 1 for axis in range(len(shape))])
    return factor_of


def bell_draw(key, extent, width, most, cuts=(), kind=jnp.bfloat16):
    factor_of = levels(key, extent, cuts, -0.22, 0.18) if cuts else 1.0
    entries = jax.random.normal(key, extent, jnp.float32) * width * factor_of
    return jnp.minimum(jnp.maximum(entries, -most), most).astype(kind)


def setup_inputs(seed: int = 0) -> dict:
    key_list = jax.random.split(jax.random.key(seed), 7)
    return {
        "outcomes": draw_outcomes(jax.random.fold_in(key_list[6], 71), 0),
        "cohort": place_ends(jax.random.randint(key_list[1], (UNITS,), 0, COHORTS + 1), jax.random.fold_in(key_list[1], 1), 0, COHORTS).astype(jnp.int32),
        "pre_end": place_ends(jax.random.randint(key_list[2], (COHORTS,), DAYS // 4, DAYS // 2), jax.random.fold_in(key_list[2], 1), DAYS // 4, (DAYS // 2) - 1).astype(jnp.int32),
        "post_start": place_ends(jax.random.randint(key_list[3], (COHORTS,), DAYS // 2, 3 * DAYS // 4), jax.random.fold_in(key_list[3], 1), DAYS // 2, (3 * DAYS // 4) - 1).astype(jnp.int32),
        "unit_logit": bell_draw(key_list[4], (COHORTS, UNITS), 0.7, 4.0, ((1, 16),), jnp.float32),
        "time_logit": bell_draw(key_list[5], (COHORTS, DAYS), 0.7, 4.0, ((1, 16),), jnp.float32),
    }


highest = lax.Precision.HIGHEST
step_rate = 16.0

def weigh_days(left, outcomes):
    return lax.dot_general(left, outcomes, (((1,), (1,)), ((), ())), precision=highest, preferred_element_type=jnp.float32)

def reference(outcomes, cohort, pre_end, post_start, unit_logit, time_logit):
    labels = jnp.arange(COHORTS, dtype=jnp.int32)[:, None]
    treated = (cohort[None, :] == labels).astype(jnp.float32)
    control = (cohort[None, :] > labels).astype(jnp.float32)
    day_index = jnp.arange(DAYS, dtype=jnp.int32)[None, :]
    before = (day_index < pre_end[:, None]).astype(jnp.float32)
    after_mask = (day_index >= post_start[:, None]).astype(jnp.float32)
    before_len = pre_end.astype(jnp.float32)
    after_len = (DAYS - post_start).astype(jnp.float32)
    raised = jnp.exp(unit_logit) * control
    unit_norm = lax.optimization_barrier(jnp.sum(raised, axis=1))
    treat_count = jnp.maximum(lax.optimization_barrier(jnp.sum(treated, axis=1)), 1.0)
    ctrl_count = lax.optimization_barrier(jnp.sum(control, axis=1))
    weights = raised / unit_norm[:, None]
    fitted = jnp.dot(weights, outcomes, precision=highest, preferred_element_type=jnp.float32)
    treat_sum = jnp.dot(treated, outcomes, precision=highest, preferred_element_type=jnp.float32)
    residual = (fitted - treat_sum / treat_count[:, None]) * before
    unit_grad = weigh_days(residual, outcomes)
    updated = weights * jnp.exp(-step_rate * unit_grad / jnp.sqrt(before_len)[:, None])
    unit_weights = updated / lax.optimization_barrier(jnp.sum(updated, axis=1))[:, None] * ctrl_count[:, None]
    time_raised = jnp.exp(time_logit) * before
    time_lam = time_raised / lax.optimization_barrier(jnp.sum(time_raised, axis=1))[:, None]
    time_fit = weigh_days(time_lam, outcomes)
    post_sum = weigh_days(after_mask, outcomes)
    shortfall = (time_fit - post_sum / after_len[:, None]) * control
    time_grad = jnp.dot(shortfall, outcomes, precision=highest, preferred_element_type=jnp.float32)
    moved = time_lam * jnp.exp(-step_rate * time_grad / jnp.sqrt(jnp.maximum(ctrl_count, 1.0))[:, None])
    time_weights = moved / lax.optimization_barrier(jnp.sum(moved, axis=1))[:, None] * before_len[:, None]
    return (unit_weights, time_weights)
```

```python
import functools

import jax
import jax.numpy as jnp
from jax import lax
from jax.experimental import pallas as pl
from jax.experimental.pallas import tpu as pltpu
from jax.sharding import PartitionSpec as P

MESH = pl.DeviceIdType.MESH
step_rate = 16.0
CHUNK = 256
LANES = 128
UNIT_SPLIT = (4, 4)
DAY_SPLIT = (4, 2, 2)
f32, bf16 = jnp.float32, jnp.bfloat16


def dot_nn(a, b):
    return jnp.dot(a, b, preferred_element_type=f32)


def dot_nt(a, b):
    return lax.dot_general(a, b, (((1,), (1,)), ((), ())), preferred_element_type=f32)


def halves(v):
    high = v.astype(bf16).astype(f32)
    return high, v - high


def to_row(col):
    groups = col.shape[0]
    row_id = lax.broadcasted_iota(jnp.int32, (groups, LANES), 0)
    lane_id = lax.broadcasted_iota(jnp.int32, (groups, LANES), 1)
    return jnp.sum(jnp.where(row_id == lane_id, col, 0.0), axis=0, keepdims=True)


def to_col(row, groups):
    row_id = lax.broadcasted_iota(jnp.int32, (groups, LANES), 0)
    lane_id = lax.broadcasted_iota(jnp.int32, (groups, LANES), 1)
    return jnp.sum(jnp.where(row_id == lane_id, row, 0.0), axis=1, keepdims=True)


def column(ref, groups):
    row_id = lax.broadcasted_iota(jnp.int32, (groups, 1), 0)
    out = jnp.zeros((groups, 1), jnp.int32)
    for g in range(groups):
        out = jnp.where(row_id == g, ref[g], out)
    return out


class Exchange:
    def __init__(self, buf, send_sem, recv_sem, rank, size, place):
        self.buf, self.send_sem, self.recv_sem = buf, send_sem, recv_sem
        self.rank, self.size, self.place = rank, size, place
        self.sent = []

    def copy(self, k, src, dst, peer):
        return pltpu.make_async_remote_copy(
            src_ref=src, dst_ref=dst, send_sem=self.send_sem.at[k - 1], recv_sem=self.recv_sem.at[k - 1],
            device_id=self.place(peer), device_id_type=MESH,
        )

    def start(self, source=None):
        own = self.buf.at[self.rank]
        for k in range(1, self.size):
            peer = lax.rem(self.rank + k, self.size)
            copy = self.copy(k, own if source is None else source.at[peer], own, peer)
            copy.start()
            self.sent.append(copy)

    def wait(self):
        for k in range(1, self.size):
            peer = lax.rem(self.rank + self.size - k, self.size)
            slot = self.buf.at[peer]
            self.copy(k, slot, slot, peer).wait_recv()

    def drain(self):
        for copy in self.sent:
            copy.wait_send()

    def total(self):
        out = self.buf[0]
        for i in range(1, self.size):
            out = out + self.buf[i]
        return out


def kernel(
    unit_split, day_split,
    pre_ref, post_ref, x_hbm, cohort_ref, unit_logit_ref, time_logit_ref,
    unit_out, time_out,
    x_buf, high_buf, low_buf, left_buf, raised_buf, control_buf,
    ux_buf, uz_buf, gx_buf, gz_buf,
    upart, urs, uzh, uag, tpart, tpost, trs, tzh, tag, lam_buf, utot, ttot,
    x_sem, ux_s, ux_r, uz_s, uz_r, gx_s, gx_r, gz_s, gz_r,
    urs_s, urs_r, uzh_s, uzh_r, uag_s, uag_r, trs_s, trs_r, tzh_s, tzh_r, tag_s, tag_r,
    lam_s, lam_r, utot_s, utot_r, ttot_s, ttot_r,
):
    nx, nz = unit_split
    ny, nh, nc = day_split
    unit_n, day_n, shards = nx * nz, ny * nh * nc, ny * nc
    units, days = x_buf.shape
    groups = unit_logit_ref.shape[0]
    chunks = units // CHUNK
    shard = units // shards
    all_count = day_n * days

    u, d = lax.axis_index("unit"), lax.axis_index("day")
    ux, uz = lax.div(u, nz), lax.rem(u, nz)
    dy, dh, dc = lax.div(d, nh * nc), lax.rem(lax.div(d, nc), nh), lax.rem(d, nc)
    j = dy * nc + dc

    loads = []
    for k in range(chunks):
        rows = pl.ds(k * CHUNK, CHUNK)
        load = pltpu.make_async_copy(x_hbm.at[rows], x_buf.at[rows], x_sem.at[k])
        load.start()
        loads.append(load)

    barrier = pltpu.get_barrier_semaphore()
    for k in range(1, unit_n):
        pl.semaphore_signal(barrier, inc=1, device_id={"unit": lax.rem(u + k, unit_n)}, device_id_type=MESH)
    for k in range(1, day_n):
        pl.semaphore_signal(barrier, inc=1, device_id={"day": lax.rem(d + k, day_n)}, device_id_type=MESH)

    def in_shards(rank):
        return {"day": lax.div(rank, nc) * (nh * nc) + dh * nc + lax.rem(rank, nc)}

    def in_high(rank):
        return {"day": dy * (nh * nc) + rank * nc + dc}

    on_x = lambda rank: {"unit": rank * nz + uz}
    on_z = lambda rank: {"unit": ux * nz + rank}
    on_unit = lambda rank: {"unit": rank}
    on_day = lambda rank: {"day": rank}

    sum_x = Exchange(ux_buf, ux_s, ux_r, ux, nx, on_x)
    sum_z = Exchange(uz_buf, uz_s, uz_r, uz, nz, on_z)
    grad_x = Exchange(gx_buf, gx_s, gx_r, ux, nx, on_x)
    grad_z = Exchange(gz_buf, gz_s, gz_r, uz, nz, on_z)
    unit_rs = Exchange(urs, urs_s, urs_r, j, shards, in_shards)
    unit_zh = Exchange(uzh, uzh_s, uzh_r, dh, nh, in_high)
    unit_ag = Exchange(uag, uag_s, uag_r, j, shards, in_shards)
    time_rs = Exchange(trs, trs_s, trs_r, j, shards, in_shards)
    time_zh = Exchange(tzh, tzh_s, tzh_r, dh, nh, in_high)
    time_ag = Exchange(tag, tag_s, tag_r, j, shards, in_shards)
    lam_tot = Exchange(lam_buf, lam_s, lam_r, d, day_n, on_day)
    unit_tot = Exchange(utot, utot_s, utot_r, u, unit_n, on_unit)
    time_tot = Exchange(ttot, ttot_s, ttot_r, d, day_n, on_day)

    pre_end, post_start = column(pre_ref, groups), column(post_ref, groups)
    before_len = pre_end.astype(f32)
    after_len = (all_count - post_start).astype(f32)
    labels = lax.broadcasted_iota(jnp.int32, (groups, units), 0)
    cohort = jnp.broadcast_to(cohort_ref[...], (groups, units))
    treated = jnp.where(cohort == labels, 1.0, 0.0)
    control = jnp.where(cohort > labels, 1.0, 0.0)
    raised = jnp.exp(unit_logit_ref[...]) * control
    for i in range(shards):
        raised_buf[i] = raised[:, i * shard:(i + 1) * shard]
        control_buf[i] = control[:, i * shard:(i + 1) * shard]
    raised_high, raised_low = halves(raised)
    left_buf[...] = jnp.concatenate(
        [raised_high, raised_low, treated, jnp.zeros_like(treated)], axis=0
    ).astype(bf16)
    norm_part = jnp.sum(raised, axis=1, keepdims=True)
    treat_part = jnp.sum(treated, axis=1, keepdims=True)
    ctrl_part = jnp.sum(control, axis=1, keepdims=True)
    lane = lax.broadcasted_iota(jnp.int32, (groups, LANES), 1)
    stats = jnp.where(lane == 0, norm_part, jnp.where(lane == 1, treat_part, jnp.where(lane == 2, ctrl_part, 0.0)))

    day_index = d * days + lax.broadcasted_iota(jnp.int32, (groups, days), 1)
    before = jnp.where(day_index < pre_end, 1.0, 0.0)
    after = jnp.where(day_index >= post_start, 1.0, 0.0)
    time_raised = jnp.exp(time_logit_ref[...]) * before
    lam_buf[d] = to_row(jnp.sum(time_raised, axis=1, keepdims=True))
    time_high, time_low = halves(time_raised)
    time_left = jnp.concatenate([time_high, time_low, after, jnp.zeros_like(after)], axis=0).astype(bf16)

    acc = jnp.zeros((4 * groups, days), f32)
    for k in range(chunks):
        rows = pl.ds(k * CHUNK, CHUNK)
        loads[k].wait()
        part = x_buf[rows, :]
        high = part.astype(bf16)
        low = (part - high.astype(f32)).astype(bf16)
        high_buf[rows, :] = high
        low_buf[rows, :] = low
        left = left_buf[:, k * CHUNK:(k + 1) * CHUNK]
        acc = acc + dot_nn(left, high) + dot_nn(left, low)
    own = ux_buf.at[ux]
    own[:, 0:days] = acc[0:groups] + acc[groups:2 * groups]
    own[:, days:2 * days] = acc[2 * groups:3 * groups]
    own[:, 2 * days:] = stats

    pl.semaphore_wait(barrier, unit_n + day_n - 2)
    sum_x.start()
    lam_tot.start()

    for k in range(chunks):
        rows = pl.ds(k * CHUNK, CHUNK)
        out = dot_nt(time_left, high_buf[rows, :]) + dot_nt(time_left, low_buf[rows, :])
        i, at = (k * CHUNK) // shard, (k * CHUNK) % shard
        tpart[i, :, at:at + CHUNK] = out[0:groups] + out[groups:2 * groups]
        tpost[i, :, at:at + CHUNK] = out[2 * groups:3 * groups]

    sum_x.wait()
    uz_buf[uz] = sum_x.total()
    sum_z.start()

    lam_tot.wait()
    lam_sum = to_col(lam_tot.total(), groups)
    tpart[...] = tpart[...] / lam_sum[None] - tpost[...] / after_len[None]
    trs[j] = tpart[j]
    time_rs.start(tpart)

    sum_z.wait()
    sums = sum_z.total()
    unit_norm = sums[:, 2 * days:2 * days + 1]
    treat_count = jnp.maximum(sums[:, 2 * days + 1:2 * days + 2], 1.0)
    ctrl_count = sums[:, 2 * days + 2:2 * days + 3]
    residual = (sums[:, 0:days] / unit_norm - sums[:, days:2 * days] / treat_count) * before
    res_left = jnp.concatenate(halves(residual), axis=0).astype(bf16)
    for k in range(chunks):
        rows = pl.ds(k * CHUNK, CHUNK)
        out = dot_nt(res_left, high_buf[rows, :]) + dot_nt(res_left, low_buf[rows, :])
        i, at = (k * CHUNK) // shard, (k * CHUNK) % shard
        upart[i, :, at:at + CHUNK] = out[0:groups] + out[groups:2 * groups]
    urs[j] = upart[j]
    unit_rs.start(upart)

    time_rs.wait()
    tzh[dh] = time_rs.total()
    time_zh.start()
    unit_rs.wait()
    uzh[dh] = unit_rs.total()
    unit_zh.start()

    time_zh.wait()
    tag[j] = time_zh.total() * control_buf[j]
    time_ag.start()
    unit_zh.wait()
    uag[j] = raised_buf[j] / unit_norm * jnp.exp(-step_rate * unit_zh.total() / jnp.sqrt(before_len))
    unit_ag.start()

    time_ag.wait()
    acc = jnp.zeros((2 * groups, days), f32)
    for k in range(chunks):
        rows = pl.ds(k * CHUNK, CHUNK)
        i, at = (k * CHUNK) // shard, (k * CHUNK) % shard
        left = jnp.concatenate(halves(tag[i, :, at:at + CHUNK]), axis=0).astype(bf16)
        acc = acc + dot_nn(left, high_buf[rows, :]) + dot_nn(left, low_buf[rows, :])
    gx_buf[ux] = acc[0:groups] + acc[groups:2 * groups]
    grad_x.start()

    unit_ag.wait()
    folded = unit_ag.total()
    utot[u] = to_row(jnp.sum(folded, axis=1, keepdims=True))
    unit_tot.start()

    grad_x.wait()
    gz_buf[uz] = grad_x.total()
    grad_z.start()

    unit_tot.wait()
    unit_total = to_col(unit_tot.total(), groups)
    for i in range(shards):
        unit_out[:, i * shard:(i + 1) * shard] = uag[i] / unit_total * ctrl_count

    grad_z.wait()
    ctrl_root = jnp.sqrt(jnp.maximum(ctrl_count, 1.0))
    moved = time_raised / lam_sum * jnp.exp(-step_rate * grad_z.total() / ctrl_root)
    ttot[d] = to_row(jnp.sum(moved, axis=1, keepdims=True))
    time_tot.start()
    time_tot.wait()
    time_out[...] = moved / to_col(time_tot.total(), groups) * before_len

    for group in (
        sum_x, lam_tot, sum_z, time_rs, unit_rs, time_zh, unit_zh, time_ag, unit_ag, grad_x, unit_tot, grad_z, time_tot
    ):
        group.drain()


def local(unit_split, day_split, outcomes, cohort, pre_end, post_start, unit_logit, time_logit):
    groups = pre_end.shape[0]
    units, days = outcomes.shape
    nx, nz = unit_split
    ny, nh, nc = day_split
    shards = ny * nc
    shard = units // shards
    wide = 2 * days + LANES
    vmem = pl.BlockSpec(memory_space=pltpu.VMEM)
    smem = pl.BlockSpec(memory_space=pltpu.SMEM)
    dma = lambda n: pltpu.SemaphoreType.DMA((n,))
    pairs = lambda *sizes: [dma(n - 1) for n in sizes for _ in range(2)]
    slots = lambda n: pltpu.VMEM((n, groups, shard), f32)
    return pl.pallas_call(
        functools.partial(kernel, unit_split, day_split),
        out_shape=(
            jax.ShapeDtypeStruct((groups, units), f32),
            jax.ShapeDtypeStruct((groups, days), f32),
        ),
        in_specs=[smem, smem, pl.BlockSpec(memory_space=pl.ANY), vmem, vmem, vmem],
        out_specs=(vmem, vmem),
        scratch_shapes=[
            pltpu.VMEM((units, days), f32),
            pltpu.VMEM((units, days), bf16),
            pltpu.VMEM((units, days), bf16),
            pltpu.VMEM((4 * groups, units), bf16),
            slots(shards), slots(shards),
            pltpu.VMEM((nx, groups, wide), f32),
            pltpu.VMEM((nz, groups, wide), f32),
            pltpu.VMEM((nx, groups, days), f32),
            pltpu.VMEM((nz, groups, days), f32),
            slots(shards), slots(shards), slots(nh), slots(shards),
            slots(shards), slots(shards), slots(shards), slots(nh), slots(shards),
            pltpu.VMEM((ny * nh * nc, 1, LANES), f32),
            pltpu.VMEM((nx * nz, 1, LANES), f32),
            pltpu.VMEM((ny * nh * nc, 1, LANES), f32),
            dma(units // CHUNK),
            *pairs(nx, nz, nx, nz),
            *pairs(shards, nh, shards, shards, nh, shards),
            *pairs(ny * nh * nc, nx * nz, ny * nh * nc),
        ],
        compiler_params=pltpu.CompilerParams(collective_id=0, has_side_effects=True),
    )(pre_end, post_start, outcomes, cohort.reshape(1, units), unit_logit, time_logit)


def solution(mesh):
    return jax.shard_map(
        functools.partial(local, UNIT_SPLIT, DAY_SPLIT),
        mesh=mesh,
        in_specs=(P("unit", "day"), P("unit"), P(), P(), P(None, "unit"), P(None, "day")),
        out_specs=(P(None, "unit"), P(None, "day")),
        check_vma=False,
    )
```

```python
import functools

import jax
import jax.numpy as jnp
from jax import lax
from jax.experimental import pallas as pl
from jax.experimental.pallas import tpu as pltpu
from jax.sharding import PartitionSpec as P

MESH = pl.DeviceIdType.MESH
step_rate = 16.0
CHUNK = 256
LANES = 128
UNIT_SPLIT = (4, 4)
DAY_SPLIT = (4, 2, 2)
f32, bf16 = jnp.float32, jnp.bfloat16


def dot_nn(a, b):
    return jnp.dot(a, b, preferred_element_type=f32)


def dot_nt(a, b):
    return lax.dot_general(a, b, (((1,), (1,)), ((), ())), preferred_element_type=f32)


def halves(v):
    high = v.astype(bf16).astype(f32)
    return high, v - high


def to_row(col):
    groups = col.shape[0]
    row_id = lax.broadcasted_iota(jnp.int32, (groups, LANES), 0)
    lane_id = lax.broadcasted_iota(jnp.int32, (groups, LANES), 1)
    return jnp.sum(jnp.where(row_id == lane_id, col, 0.0), axis=0, keepdims=True)


def to_col(row, groups):
    row_id = lax.broadcasted_iota(jnp.int32, (groups, LANES), 0)
    lane_id = lax.broadcasted_iota(jnp.int32, (groups, LANES), 1)
    return jnp.sum(jnp.where(row_id == lane_id, row, 0.0), axis=1, keepdims=True)


def column(ref, groups):
    row_id = lax.broadcasted_iota(jnp.int32, (groups, 1), 0)
    out = jnp.zeros((groups, 1), jnp.int32)
    for g in range(groups):
        out = jnp.where(row_id == g, ref[g], out)
    return out


class Exchange:
    def __init__(self, buf, send_sem, recv_sem, rank, size, place, sends=None, takes=None):
        self.buf, self.send_sem, self.recv_sem = buf, send_sem, recv_sem
        self.rank, self.size, self.place = rank, size, place
        self.sends, self.takes = sends, takes

    def copy(self, k, src, dst, peer):
        return pltpu.make_async_remote_copy(
            src_ref=src, dst_ref=dst, send_sem=self.send_sem.at[k - 1], recv_sem=self.recv_sem.at[k - 1],
            device_id=self.place(peer), device_id_type=MESH,
        )

    def over_sends(self, act):
        for k in range(1, self.size):
            peer = lax.rem(self.rank + k, self.size)
            if self.takes is None:
                act(k, peer)
            else:
                pl.when(self.takes(peer))(functools.partial(act, k, peer))

    def start(self, source=None):
        own = self.buf.at[self.rank]

        def act(k, peer):
            self.copy(k, own if source is None else source.at[peer], own, peer).start()

        self.over_sends(act)

    def drain(self):
        own = self.buf.at[self.rank]
        self.over_sends(lambda k, peer: self.copy(k, own, own, peer).wait_send())

    def wait(self):
        for k in range(1, self.size):
            peer = lax.rem(self.rank + self.size - k, self.size)

            def act(k=k, peer=peer):
                slot = self.buf.at[peer]
                self.copy(k, slot, slot, peer).wait_recv()

            if self.sends is None:
                act()
            else:
                pl.when(self.sends(peer))(act)

    def total(self, low=0, high=None):
        out = self.buf[low]
        for i in range(low + 1, self.size if high is None else high):
            out = out + self.buf[i]
        return out


def kernel(
    unit_split, day_split,
    pre_hbm, post_hbm, x_hbm, cohort_hbm, unit_logit_hbm, time_logit_hbm,
    unit_out, time_out,
    pre_ref, post_ref, cohort_ref, unit_logit_ref, time_logit_ref,
    x_buf, high_buf, low_buf, left_buf, raised_buf, control_buf, moved_buf, stat_buf,
    ux_buf, uz_buf, gx_buf, gz_buf,
    upart, urs, uzh, uag, tpart, trs, tzh, tag, utot, ttot,
    in_sem, x_sem, ux_s, ux_r, uz_s, uz_r, gx_s, gx_r, gz_s, gz_r,
    urs_s, urs_r, uzh_s, uzh_r, uag_s, uag_r, trs_s, trs_r, tzh_s, tzh_r, tag_s, tag_r,
    utot_s, utot_r, ttot_s, ttot_r,
):
    nx, nz = unit_split
    ny, nh, nc = day_split
    unit_n, day_n, shards = nx * nz, ny * nh * nc, ny * nc
    units, days = x_buf.shape
    groups = unit_logit_ref.shape[0]
    chunks = units // CHUNK
    shard = units // shards
    all_count = day_n * days
    early_ranks, early_days = shards // 2, day_n // 2

    u, d = lax.axis_index("unit"), lax.axis_index("day")
    ux, uz = lax.div(u, nz), lax.rem(u, nz)
    dy, dh, dc = lax.div(d, nh * nc), lax.rem(lax.div(d, nc), nh), lax.rem(d, nc)
    j = dy * nc + dc
    early = j < early_ranks

    barrier = pltpu.get_barrier_semaphore()
    for k in range(1, unit_n):
        pl.semaphore_signal(barrier, inc=1, device_id={"unit": lax.rem(u + k, unit_n)}, device_id_type=MESH)
    for k in range(1, day_n):
        pl.semaphore_signal(barrier, inc=1, device_id={"day": lax.rem(d + k, day_n)}, device_id_type=MESH)

    inputs = []
    for k, (src, dst) in enumerate((
        (time_logit_hbm, time_logit_ref), (pre_hbm, pre_ref), (post_hbm, post_ref),
        (unit_logit_hbm, unit_logit_ref), (cohort_hbm, cohort_ref),
    )):
        inputs.append(pltpu.make_async_copy(src, dst, in_sem.at[k]))
    loads = []
    for k in range(chunks):
        rows = pl.ds(k * CHUNK, CHUNK)
        loads.append(pltpu.make_async_copy(x_hbm.at[rows], x_buf.at[rows], x_sem.at[k]))
    for copy in inputs[:3] + loads[:2] + inputs[3:] + loads[2:]:
        copy.start()

    def in_shards(rank):
        return {"day": lax.div(rank, nc) * (nh * nc) + dh * nc + lax.rem(rank, nc)}

    def in_high(rank):
        return {"day": dy * (nh * nc) + rank * nc + dc}

    on_x = lambda rank: {"unit": rank * nz + uz}
    on_z = lambda rank: {"unit": ux * nz + rank}
    on_unit = lambda rank: {"unit": rank}
    on_day = lambda rank: {"day": rank}
    is_early = lambda rank: rank < early_ranks

    sum_x = Exchange(ux_buf, ux_s, ux_r, ux, nx, on_x)
    sum_z = Exchange(uz_buf, uz_s, uz_r, uz, nz, on_z)
    grad_x = Exchange(gx_buf, gx_s, gx_r, ux, nx, on_x)
    grad_z = Exchange(gz_buf, gz_s, gz_r, uz, nz, on_z)
    unit_rs = Exchange(urs, urs_s, urs_r, j, shards, in_shards, sends=is_early)
    unit_zh = Exchange(uzh, uzh_s, uzh_r, dh, nh, in_high)
    unit_ag = Exchange(uag, uag_s, uag_r, j, shards, in_shards)
    time_rs = Exchange(trs, trs_s, trs_r, j, shards, in_shards)
    time_zh = Exchange(tzh, tzh_s, tzh_r, dh, nh, in_high)
    time_ag = Exchange(tag, tag_s, tag_r, j, shards, in_shards, takes=is_early)
    unit_tot = Exchange(utot, utot_s, utot_r, u, unit_n, on_unit)
    time_tot = Exchange(ttot, ttot_s, ttot_r, d, early_days, on_day)

    for copy in inputs[:3]:
        copy.wait()
    pre_end, post_start = column(pre_ref, groups), column(post_ref, groups)
    before_len = pre_end.astype(f32)
    after_len = (all_count - post_start).astype(f32)
    day_index = d * days + lax.broadcasted_iota(jnp.int32, (groups, days), 1)
    before = jnp.where(day_index < pre_end, 1.0, 0.0)
    after = jnp.where(day_index >= post_start, 1.0, 0.0)
    time_raised = jnp.exp(time_logit_ref[...]) * before
    moved_buf[...] = time_raised
    time_left = jnp.concatenate(halves(time_raised + after), axis=0).astype(bf16)
    scale = jnp.where(early, 1.0, 1.0 / after_len)
    lam_tile = jnp.broadcast_to(jnp.sum(time_raised, axis=1, keepdims=True), (groups, LANES))
    for i in range(shards):
        tpart[i, :, shard:] = lam_tile
    for k in range(chunks):
        rows = pl.ds(k * CHUNK, CHUNK)
        loads[k].wait()
        part = x_buf[rows, :]
        high = part.astype(bf16)
        low = (part - high.astype(f32)).astype(bf16)
        high_buf[rows, :] = high
        low_buf[rows, :] = low
        out = dot_nt(time_left, high) + dot_nt(time_left, low)
        i, at = (k * CHUNK) // shard, (k * CHUNK) % shard
        tpart[i, :, at:at + CHUNK] = (out[0:groups] + out[groups:]) * scale

    pl.semaphore_wait(barrier, unit_n + day_n - 2)
    trs[j] = tpart[j]
    time_rs.start(tpart)

    for copy in inputs[3:]:
        copy.wait()
    labels = lax.broadcasted_iota(jnp.int32, (groups, units), 0)
    cohort = jnp.broadcast_to(cohort_ref[...], (groups, units))
    treated = jnp.where(cohort == labels, 1.0, 0.0)
    control = jnp.where(cohort > labels, 1.0, 0.0)
    raised = jnp.exp(unit_logit_ref[...]) * control
    for i in range(shards):
        raised_buf[i] = raised[:, i * shard:(i + 1) * shard]
        control_buf[i] = control[:, i * shard:(i + 1) * shard]

    @pl.when(early)
    def _():
        raised_high, raised_low = halves(raised)
        left_buf[...] = jnp.concatenate(
            [raised_high, raised_low, treated, jnp.zeros_like(treated)], axis=0
        ).astype(bf16)
        norm_part = jnp.sum(raised, axis=1, keepdims=True)
        treat_part = jnp.sum(treated, axis=1, keepdims=True)
        ctrl_part = jnp.sum(control, axis=1, keepdims=True)
        lane = lax.broadcasted_iota(jnp.int32, (groups, LANES), 1)
        stats = jnp.where(
            lane == 0, norm_part, jnp.where(lane == 1, treat_part, jnp.where(lane == 2, ctrl_part, 0.0))
        )
        acc = dot_nn(left_buf[...], high_buf[...]) + dot_nn(left_buf[...], low_buf[...])
        own = ux_buf.at[ux]
        own[:, 0:days] = acc[0:groups] + acc[groups:2 * groups]
        own[:, days:2 * days] = acc[2 * groups:3 * groups]
        own[:, 2 * days:] = stats
        sum_x.start()

    time_rs.wait()
    own_zh = tzh.at[dh]
    own_zh[0] = time_rs.total(0, early_ranks)
    own_zh[1] = time_rs.total(early_ranks, shards)
    time_zh.start()

    @pl.when(early)
    def _():
        sum_x.wait()
        uz_buf[uz] = sum_x.total()
        sum_z.start()

    time_zh.wait()
    both = time_zh.total()
    lam_owner = both[0, :, shard:shard + 1]
    own_ag = tag.at[j]
    own_ag[:, 0:shard] = (both[0, :, 0:shard] / lam_owner - both[1, :, 0:shard]) * control_buf[j]
    own_ag[:, shard:] = both[0, :, shard:]
    time_ag.start()

    @pl.when(early)
    def _():
        sum_z.wait()
        sums = sum_z.total()
        unit_norm = sums[:, 2 * days:2 * days + 1]
        treat_count = jnp.maximum(sums[:, 2 * days + 1:2 * days + 2], 1.0)
        residual = (sums[:, 0:days] / unit_norm - sums[:, days:2 * days] / treat_count) * before
        res_left = jnp.concatenate(halves(residual), axis=0).astype(bf16)
        for i in range(shards):
            rows = pl.ds(i * shard, shard)
            out = dot_nt(res_left, high_buf[rows, :]) + dot_nt(res_left, low_buf[rows, :])
            upart[i, :, 0:shard] = out[0:groups] + out[groups:]
            upart[i, :, shard:] = sums[:, 2 * days:]
        urs[j] = upart[j]
        unit_rs.start(upart)

    @pl.when(early)
    def _():
        time_ag.wait()
        for i in range(shards):
            left_buf[0:2 * groups, i * shard:(i + 1) * shard] = jnp.concatenate(
                halves(tag[i, :, 0:shard]), axis=0
            ).astype(bf16)
        left = left_buf[0:2 * groups, :]
        acc = dot_nn(left, high_buf[...]) + dot_nn(left, low_buf[...])
        gx_buf[ux] = acc[0:groups] + acc[groups:]
        grad_x.start()

    unit_rs.wait()
    grads = unit_rs.total(0, early_ranks)
    uzh[dh] = grads[:, 0:shard]
    stat_buf[...] = urs[0, :, shard:]
    unit_zh.start()

    @pl.when(early)
    def _():
        grad_x.wait()
        gz_buf[uz] = grad_x.total()
        grad_z.start()

    unit_zh.wait()
    unit_norm = stat_buf[:, 0:1]
    ctrl_count = stat_buf[:, 2:3]
    uag[j] = raised_buf[j] / unit_norm * jnp.exp(-step_rate * unit_zh.total() / jnp.sqrt(before_len))
    unit_ag.start()

    @pl.when(early)
    def _():
        grad_z.wait()
        lam = moved_buf[...] / tag[0, :, shard:shard + 1]
        ctrl_root = jnp.sqrt(jnp.maximum(ctrl_count, 1.0))
        moved = lam * jnp.exp(-step_rate * grad_z.total() / ctrl_root)
        moved_buf[...] = moved
        ttot[d] = to_row(jnp.sum(moved, axis=1, keepdims=True))
        time_tot.start()

    unit_ag.wait()
    utot[u] = to_row(jnp.sum(unit_ag.total(), axis=1, keepdims=True))
    unit_tot.start()

    unit_tot.wait()
    unit_total = to_col(unit_tot.total(), groups)
    for i in range(shards):
        unit_out[:, i * shard:(i + 1) * shard] = uag[i] / unit_total * ctrl_count

    @pl.when(early)
    def _():
        time_tot.wait()
        time_out[...] = moved_buf[...] / to_col(time_tot.total(), groups) * before_len

    @pl.when(jnp.logical_not(early))
    def _():
        time_out[...] = jnp.zeros_like(time_out)

    for group in (time_rs, time_zh, time_ag, unit_zh, unit_ag, unit_tot):
        group.drain()

    @pl.when(early)
    def _():
        for group in (sum_x, sum_z, unit_rs, grad_x, grad_z, time_tot):
            group.drain()


def local(unit_split, day_split, outcomes, cohort, pre_end, post_start, unit_logit, time_logit):
    groups = pre_end.shape[0]
    units, days = outcomes.shape
    nx, nz = unit_split
    ny, nh, nc = day_split
    unit_n, day_n, shards = nx * nz, ny * nh * nc, ny * nc
    shard = units // shards
    wide = 2 * days + LANES
    vmem = pl.BlockSpec(memory_space=pltpu.VMEM)
    hbm = pl.BlockSpec(memory_space=pl.ANY)
    dma = lambda n: pltpu.SemaphoreType.DMA((n,))
    pairs = lambda *sizes: [dma(n - 1) for n in sizes for _ in range(2)]
    slots = lambda n, size: pltpu.VMEM((n, groups, size), f32)
    return pl.pallas_call(
        functools.partial(kernel, unit_split, day_split),
        out_shape=(
            jax.ShapeDtypeStruct((groups, units), f32),
            jax.ShapeDtypeStruct((groups, days), f32),
        ),
        in_specs=[hbm] * 6,
        out_specs=(vmem, vmem),
        scratch_shapes=[
            pltpu.SMEM((groups,), jnp.int32),
            pltpu.SMEM((groups,), jnp.int32),
            pltpu.VMEM((1, units), jnp.int32),
            pltpu.VMEM((groups, units), f32),
            pltpu.VMEM((groups, days), f32),
            pltpu.VMEM((units, days), f32),
            pltpu.VMEM((units, days), bf16),
            pltpu.VMEM((units, days), bf16),
            pltpu.VMEM((4 * groups, units), bf16),
            slots(shards, shard), slots(shards, shard),
            pltpu.VMEM((groups, days), f32),
            pltpu.VMEM((groups, LANES), f32),
            slots(nx, wide), slots(nz, wide), slots(nx, days), slots(nz, days),
            slots(shards, shard + LANES), slots(shards, shard + LANES), slots(nh, shard), slots(shards, shard),
            slots(shards, shard + LANES), slots(shards, shard + LANES),
            pltpu.VMEM((nh, 2, groups, shard + LANES), f32),
            slots(shards, shard + LANES),
            pltpu.VMEM((unit_n, 1, LANES), f32),
            pltpu.VMEM((day_n // 2, 1, LANES), f32),
            dma(5),
            dma(units // CHUNK),
            *pairs(nx, nz, nx, nz),
            *pairs(shards, nh, shards, shards, nh, shards),
            *pairs(unit_n, day_n // 2),
        ],
        compiler_params=pltpu.CompilerParams(collective_id=0, has_side_effects=True),
    )(pre_end, post_start, outcomes, cohort.reshape(1, units), unit_logit, time_logit)


def solution(mesh):
    return jax.shard_map(
        functools.partial(local, UNIT_SPLIT, DAY_SPLIT),
        mesh=mesh,
        in_specs=(P("unit", "day"), P("unit"), P(), P(), P(None, "unit"), P(None, "day")),
        out_specs=(P(None, "unit"), P(None, "day")),
        check_vma=False,
    )
```

```python
import functools

import jax
import jax.numpy as jnp
from jax import lax
from jax.experimental import pallas as pl
from jax.experimental.pallas import tpu as pltpu
from jax.sharding import PartitionSpec as P

MESH = pl.DeviceIdType.MESH
step_rate = 16.0
CHUNK = 256
LANES = 128
UNIT_SPLIT = (4, 4)
DAY_SPLIT = (4, 2, 2)
f32, bf16 = jnp.float32, jnp.bfloat16


def dot_nn(a, b):
    return jnp.dot(a, b, preferred_element_type=f32)


def dot_nt(a, b):
    return lax.dot_general(a, b, (((1,), (1,)), ((), ())), preferred_element_type=f32)


def halves(v):
    high = v.astype(bf16).astype(f32)
    return high, v - high


def to_row(col):
    groups = col.shape[0]
    row_id = lax.broadcasted_iota(jnp.int32, (groups, LANES), 0)
    lane_id = lax.broadcasted_iota(jnp.int32, (groups, LANES), 1)
    return jnp.sum(jnp.where(row_id == lane_id, col, 0.0), axis=0, keepdims=True)


def to_col(row, groups):
    row_id = lax.broadcasted_iota(jnp.int32, (groups, LANES), 0)
    lane_id = lax.broadcasted_iota(jnp.int32, (groups, LANES), 1)
    return jnp.sum(jnp.where(row_id == lane_id, row, 0.0), axis=1, keepdims=True)


def column(ref, groups):
    row_id = lax.broadcasted_iota(jnp.int32, (groups, 1), 0)
    out = jnp.zeros((groups, 1), jnp.int32)
    for g in range(groups):
        out = jnp.where(row_id == g, ref[g], out)
    return out


class Exchange:
    def __init__(self, buf, sems, rank, size, place, takes=None, flag=None, sent=None, taken=None):
        self.buf, self.sems = buf, sems
        self.rank, self.size, self.place = rank, size, place
        self.takes, self.flag = takes, flag
        self.sent = size - 1 if sent is None else sent
        self.taken = size - 1 if taken is None else taken

    def copy(self, src, dst, peer):
        return pltpu.make_async_remote_copy(
            src_ref=src, dst_ref=dst, send_sem=self.sems.at[0], recv_sem=self.sems.at[1],
            device_id=self.place(peer), device_id_type=MESH,
        )

    def start(self, source=None):
        own = self.buf.at[self.rank]
        for k in range(1, self.size):
            peer = lax.rem(self.rank + k, self.size)

            def act(peer=peer):
                self.copy(own if source is None else source.at[peer], own, peer).start()

            if self.takes is None:
                act()
            else:
                pl.when(self.takes(peer))(act)

    def all_of(self, count, act):
        def some(n):
            if n:
                slots = self.buf.at[pl.ds(0, n)]
                act(self.copy(slots, slots, lax.rem(self.rank + 1, self.size)))

        if isinstance(count, tuple):
            pl.when(self.flag)(lambda: some(count[0]))
            pl.when(jnp.logical_not(self.flag))(lambda: some(count[1]))
        else:
            some(count)

    def drain(self):
        self.all_of(self.sent, lambda copy: copy.wait_send())

    def wait(self):
        self.all_of(self.taken, lambda copy: copy.wait_recv())

    def total(self, low=0, high=None):
        out = self.buf[low]
        for i in range(low + 1, self.size if high is None else high):
            out = out + self.buf[i]
        return out


def kernel(
    unit_split, day_split,
    pre_hbm, post_hbm, x_hbm, cohort_hbm, unit_logit_hbm, time_logit_hbm,
    unit_out, time_out,
    pre_ref, post_ref, cohort_ref, unit_logit_ref, time_logit_ref,
    x_buf, high_buf, low_buf, high_turned, low_turned, left_buf, raised_buf, control_buf, moved_buf,
    stat_buf, ux_buf, uz_buf, grad,
    upart, urs, uzh, uag, tpart, trs, tzh, tag, lrs, lzh, utot, uall, ttot,
    in_sem, x_sem, stat_sem, ux_sem, uz_sem, grad_sem,
    urs_sem, uzh_sem, uag_sem, trs_sem, tzh_sem, tag_sem, lrs_sem, lzh_sem, utot_sem, uall_sem, ttot_sem,
):
    nx, nz = unit_split
    ny, nh, nc = day_split
    unit_n, day_n, shards = nx * nz, ny * nh * nc, ny * nc
    units, days = x_buf.shape
    groups = unit_logit_ref.shape[0]
    chunks = units // CHUNK
    shard = units // shards
    all_count = day_n * days
    early_ranks, early_days = shards // 2, day_n // 2

    u, d = lax.axis_index("unit"), lax.axis_index("day")
    ux, uz = lax.div(u, nz), lax.rem(u, nz)
    dy, dh, dc = lax.div(d, nh * nc), lax.rem(lax.div(d, nc), nh), lax.rem(d, nc)
    j = dy * nc + dc
    early = j < early_ranks

    def in_shards(rank):
        return {"day": lax.div(rank, nc) * (nh * nc) + dh * nc + lax.rem(rank, nc)}

    def in_high(rank):
        return {"day": dy * (nh * nc) + rank * nc + dc}

    on_unit = lambda rank: {"unit": rank}
    on_day = lambda rank: {"day": rank}
    on_x = lambda rank: {"unit": rank * nz + uz}
    on_z = lambda rank: {"unit": ux * nz + rank}

    barrier = pltpu.get_barrier_semaphore()
    for k in range(1, unit_n):
        pl.semaphore_signal(barrier, inc=1, device_id=on_unit(lax.rem(u + k, unit_n)), device_id_type=MESH)
    for k in range(1, shards):
        pl.semaphore_signal(barrier, inc=1, device_id=in_shards(lax.rem(j + k, shards)), device_id_type=MESH)
    for k in range(1, nh):
        for i in range(early_ranks):
            peer = lax.rem(dh + k, nh) * nc + i // nc * nh * nc + i % nc

            @pl.when(early)
            def _(peer=peer):
                pl.semaphore_signal(barrier, inc=1, device_id=on_day(peer), device_id_type=MESH)

        @pl.when(jnp.logical_not(early))
        def _(k=k):
            pl.semaphore_signal(barrier, inc=1, device_id=in_high(lax.rem(dh + k, nh)), device_id_type=MESH)

    inputs = []
    for k, (src, dst) in enumerate((
        (time_logit_hbm, time_logit_ref), (pre_hbm, pre_ref), (post_hbm, post_ref),
        (unit_logit_hbm, unit_logit_ref), (cohort_hbm, cohort_ref),
    )):
        inputs.append(pltpu.make_async_copy(src, dst, in_sem.at[k]))
    loads = []
    for k in range(chunks):
        rows = pl.ds(k * CHUNK, CHUNK)
        loads.append(pltpu.make_async_copy(x_hbm.at[rows], x_buf.at[rows], x_sem.at[k]))
    for copy in inputs[:3] + loads + inputs[3:]:
        copy.start()

    stats = Exchange(stat_buf, stat_sem, u, unit_n, on_unit)
    sum_x = Exchange(ux_buf, ux_sem, ux, nx, on_x)
    sum_z = Exchange(uz_buf, uz_sem, uz, nz, on_z)
    to_early = (early_ranks - 1, early_ranks)
    from_early = dict(flag=early, taken=to_early)
    unit_rs = Exchange(urs, urs_sem, j, shards, in_shards, **from_early)
    unit_zh = Exchange(uzh, uzh_sem, dh, nh, in_high)
    unit_ag = Exchange(uag, uag_sem, j, shards, in_shards)
    unit_tot = Exchange(utot, utot_sem, u, unit_n, on_unit)
    unit_all = Exchange(uall, uall_sem, j, shards, in_shards)
    time_rs = Exchange(trs, trs_sem, j, shards, in_shards)
    time_zh = Exchange(tzh, tzh_sem, dh, nh, in_high)
    time_ag = Exchange(
        tag, tag_sem, j, shards, in_shards, takes=lambda rank: rank < early_ranks, flag=early, sent=to_early
    )
    lam_rs = Exchange(lrs, lrs_sem, j, shards, in_shards, **from_early)
    lam_zh = Exchange(lzh, lzh_sem, dh, nh, in_high)
    time_grad = Exchange(grad, grad_sem, u, unit_n, on_unit)
    time_tot = Exchange(ttot, ttot_sem, d, early_days, on_day)

    def split(k):
        rows = pl.ds(k * CHUNK, CHUNK)
        part = x_buf[rows, :]
        high = part.astype(bf16)
        high_buf[rows, :] = high
        low_buf[rows, :] = (part - high.astype(f32)).astype(bf16)

    half = chunks // 2
    for k in range(half):
        loads[k].wait()
        split(k)
    for copy in inputs[:3]:
        copy.wait()
    pre_end, post_start = column(pre_ref, groups), column(post_ref, groups)
    before_len = pre_end.astype(f32)
    after_len = (all_count - post_start).astype(f32)
    day_index = d * days + lax.broadcasted_iota(jnp.int32, (groups, days), 1)
    before = jnp.where(day_index < pre_end, 1.0, 0.0)
    after = jnp.where(day_index >= post_start, 1.0, 0.0)
    time_raised = jnp.exp(time_logit_ref[...]) * before
    moved_buf[...] = time_raised
    time_left = jnp.concatenate(halves(time_raised + after), axis=0).astype(bf16)
    scale = jnp.broadcast_to(jnp.where(early, 1.0, 1.0 / after_len), (groups, CHUNK))
    lrs[j] = to_row(jnp.sum(time_raised, axis=1, keepdims=True))

    def weigh(k):
        rows = pl.ds(k * CHUNK, CHUNK)
        out = dot_nt(time_left, high_buf[rows, :]) + dot_nt(time_left, low_buf[rows, :])
        i, at = (k * CHUNK) // shard, (k * CHUNK) % shard
        tpart[i, :, at:at + CHUNK] = (out[0:groups] + out[groups:]) * scale

    for k in range(half, chunks):
        loads[k].wait()
    for k in range(half):
        weigh(k)
        split(half + k)
    for k in range(half, chunks):
        weigh(k)

    pl.semaphore_wait(
        barrier, unit_n - 1 + shards - 1 + jnp.where(early, (nh - 1) * early_ranks, nh - 1)
    )
    trs[j] = tpart[j]
    time_rs.start(tpart)

    @pl.when(early)
    def _():
        lam_rs.start()

    for copy in inputs[3:]:
        copy.wait()
    labels = lax.broadcasted_iota(jnp.int32, (groups, units), 0)
    cohort = jnp.broadcast_to(cohort_ref[...], (groups, units))
    treated = jnp.where(cohort == labels, 1.0, 0.0)
    control = jnp.where(cohort > labels, 1.0, 0.0)
    raised = jnp.exp(unit_logit_ref[...]) * control
    for i in range(shards):
        raised_buf[i] = raised[:, i * shard:(i + 1) * shard]
        control_buf[i] = control[:, i * shard:(i + 1) * shard]
    norm_part = jnp.sum(raised, axis=1, keepdims=True)
    treat_part = jnp.sum(treated, axis=1, keepdims=True)
    ctrl_part = jnp.sum(control, axis=1, keepdims=True)
    rows3 = [to_row(norm_part), to_row(treat_part), to_row(ctrl_part)]
    stat_buf[u] = jnp.concatenate(rows3 + [jnp.zeros((groups - 3, LANES), f32)], axis=0)
    stats.start()

    @pl.when(early)
    def _():
        raised_high, raised_low = halves(raised)
        left_buf[...] = jnp.concatenate(
            [raised_high, raised_low, treated, jnp.zeros_like(treated)], axis=0
        ).astype(bf16)
        acc = dot_nn(left_buf[...], high_buf[...]) + dot_nn(left_buf[...], low_buf[...])
        ux_buf[ux, :, 0:days] = acc[0:groups] + acc[groups:2 * groups]
        ux_buf[ux, :, days:] = acc[2 * groups:3 * groups]
        sum_x.start()
        for k in range(chunks):
            rows = pl.ds(k * CHUNK, CHUNK)
            high_turned[:, k * CHUNK:(k + 1) * CHUNK] = high_buf[rows, :].T
            low_turned[:, k * CHUNK:(k + 1) * CHUNK] = low_buf[rows, :].T

    time_rs.wait()
    tzh[dh, 0] = time_rs.total(0, early_ranks)
    tzh[dh, 1] = time_rs.total(early_ranks, shards)
    time_zh.start()
    lam_rs.wait()
    lzh[dh] = lam_rs.total(0, early_ranks)
    lam_zh.start()

    @pl.when(early)
    def _():
        sum_x.wait()
        uz_buf[uz] = sum_x.total()
        sum_z.start()

    stats.wait()
    all_stats = stats.total()
    unit_norm = to_col(all_stats[0:1], groups)
    treat_count = jnp.maximum(to_col(all_stats[1:2], groups), 1.0)
    ctrl_count = to_col(all_stats[2:3], groups)

    @pl.when(early)
    def _():
        sum_z.wait()
        sums = sum_z.total()
        residual = (sums[:, 0:days] / unit_norm - sums[:, days:] / treat_count) * before
        res_left = jnp.concatenate(halves(residual), axis=0).astype(bf16)
        for i in range(shards):
            cols = slice(i * shard, (i + 1) * shard)
            out = dot_nn(res_left, high_turned[:, cols]) + dot_nn(res_left, low_turned[:, cols])
            upart[i] = out[0:groups] + out[groups:]
        urs[j] = upart[j]
        unit_rs.start(upart)

    time_zh.wait()
    lam_zh.wait()
    lam_sum = to_col(lam_zh.total(), groups)
    both = time_zh.total()
    tag[j] = (both[0] / lam_sum - both[1]) * control_buf[j]
    time_ag.start()

    unit_rs.wait()
    uzh[dh] = unit_rs.total(0, early_ranks)
    unit_zh.start()

    @pl.when(early)
    def _():
        time_ag.wait()
        for i in range(shards):
            left_buf[0:2 * groups, i * shard:(i + 1) * shard] = jnp.concatenate(
                halves(tag[i]), axis=0
            ).astype(bf16)
        left = left_buf[0:2 * groups, :]
        acc = dot_nn(left, high_buf[...]) + dot_nn(left, low_buf[...])
        grad[u] = acc[0:groups] + acc[groups:]
        time_grad.start()

    unit_zh.wait()
    updated = raised_buf[j] / unit_norm * jnp.exp(-step_rate * unit_zh.total() / jnp.sqrt(before_len))
    uag[j] = updated
    utot[u] = to_row(jnp.sum(updated, axis=1, keepdims=True))
    unit_tot.start()
    unit_ag.start()

    @pl.when(early)
    def _():
        time_grad.wait()
        ctrl_root = jnp.sqrt(jnp.maximum(ctrl_count, 1.0))
        moved = moved_buf[...] / lam_sum * jnp.exp(-step_rate * time_grad.total() / ctrl_root)
        moved_buf[...] = moved
        ttot[d] = to_row(jnp.sum(moved, axis=1, keepdims=True))
        time_tot.start()

    unit_tot.wait()
    uall[j] = unit_tot.total()
    unit_all.start()

    unit_ag.wait()
    unit_all.wait()
    unit_total = jnp.broadcast_to(to_col(unit_all.total(), groups), (groups, shard))
    count = jnp.broadcast_to(ctrl_count, (groups, shard))
    for i in range(shards):
        unit_out[:, i * shard:(i + 1) * shard] = uag[i] / unit_total * count

    @pl.when(early)
    def _():
        time_tot.wait()
        time_out[...] = moved_buf[...] / to_col(time_tot.total(), groups) * before_len

    @pl.when(jnp.logical_not(early))
    def _():
        time_out[...] = jnp.zeros_like(time_out)

    for group in (time_rs, stats, time_zh, lam_zh, time_ag, unit_zh, unit_ag, unit_tot, unit_all):
        group.drain()

    @pl.when(early)
    def _():
        for group in (lam_rs, sum_x, sum_z, unit_rs, time_grad, time_tot):
            group.drain()


def local(unit_split, day_split, outcomes, cohort, pre_end, post_start, unit_logit, time_logit):
    groups = pre_end.shape[0]
    units, days = outcomes.shape
    nx, nz = unit_split
    ny, nh, nc = day_split
    unit_n, day_n, shards = nx * nz, ny * nh * nc, ny * nc
    shard = units // shards
    hbm = pl.BlockSpec(memory_space=pl.ANY)
    vmem = pl.BlockSpec(memory_space=pltpu.VMEM)
    dma = lambda n: pltpu.SemaphoreType.DMA((n,))
    slots = lambda n, size: pltpu.VMEM((n, groups, size), f32)
    rows = lambda n: pltpu.VMEM((n, 1, LANES), f32)
    return pl.pallas_call(
        functools.partial(kernel, unit_split, day_split),
        out_shape=(pltpu.VMEM((groups, units), f32), pltpu.VMEM((groups, days), f32)),
        in_specs=[hbm] * 6,
        out_specs=(vmem, vmem),
        scratch_shapes=[
            pltpu.SMEM((groups,), jnp.int32),
            pltpu.SMEM((groups,), jnp.int32),
            pltpu.VMEM((1, units), jnp.int32),
            pltpu.VMEM((groups, units), f32),
            pltpu.VMEM((groups, days), f32),
            pltpu.VMEM((units, days), f32),
            pltpu.VMEM((units, days), bf16),
            pltpu.VMEM((units, days), bf16),
            pltpu.VMEM((days, units), bf16),
            pltpu.VMEM((days, units), bf16),
            pltpu.VMEM((4 * groups, units), bf16),
            slots(shards, shard), slots(shards, shard),
            pltpu.VMEM((groups, days), f32),
            slots(unit_n, LANES), slots(nx, 2 * days), slots(nz, 2 * days), slots(unit_n, days),
            slots(shards, shard), slots(shards, shard), slots(nh, shard), slots(shards, shard),
            slots(shards, shard), slots(shards, shard),
            pltpu.VMEM((nh, 2, groups, shard), f32),
            slots(shards, shard),
            rows(shards), rows(nh), rows(unit_n), rows(shards), rows(day_n // 2),
            dma(5),
            dma(units // CHUNK),
            *[dma(2)] * 15,
        ],
        compiler_params=pltpu.CompilerParams(collective_id=0, has_side_effects=True),
    )(pre_end, post_start, outcomes, cohort.reshape(1, units), unit_logit, time_logit)


def solution(mesh):
    return jax.shard_map(
        functools.partial(local, UNIT_SPLIT, DAY_SPLIT),
        mesh=mesh,
        in_specs=(P("unit", "day"), P("unit"), P(), P(), P(None, "unit"), P(None, "day")),
        out_specs=(P(None, "unit"), P(None, "day")),
        check_vma=False,
    )
```

```python
import functools

import jax
import jax.numpy as jnp
from jax import lax
from jax.experimental import pallas as pl
from jax.experimental.pallas import tpu as pltpu
from jax.sharding import PartitionSpec as P

MESH = pl.DeviceIdType.MESH
step_rate = 16.0
CHUNK = 256
PARTS = 4
LANES = 128
UNIT_SPLIT = (4, 4)
DAY_SPLIT = (4, 2, 2)
f32, bf16 = jnp.float32, jnp.bfloat16


def dot_nn(a, b):
    return jnp.dot(a, b, preferred_element_type=f32)


def dot_nt(a, b):
    return lax.dot_general(a, b, (((1,), (1,)), ((), ())), preferred_element_type=f32)


def halves(v):
    high = v.astype(bf16).astype(f32)
    return high, v - high


def to_row(col):
    groups = col.shape[0]
    row_id = lax.broadcasted_iota(jnp.int32, (groups, LANES), 0)
    lane_id = lax.broadcasted_iota(jnp.int32, (groups, LANES), 1)
    return jnp.sum(jnp.where(row_id == lane_id, col, 0.0), axis=0, keepdims=True)


def to_col(row, groups):
    row_id = lax.broadcasted_iota(jnp.int32, (groups, LANES), 0)
    lane_id = lax.broadcasted_iota(jnp.int32, (groups, LANES), 1)
    return jnp.sum(jnp.where(row_id == lane_id, row, 0.0), axis=1, keepdims=True)


def column(ref, groups):
    row_id = lax.broadcasted_iota(jnp.int32, (groups, 1), 0)
    out = jnp.zeros((groups, 1), jnp.int32)
    for g in range(groups):
        out = jnp.where(row_id == g, ref[g], out)
    return out


class Exchange:
    def __init__(self, buf, sems, rank, size, place, takes=None, flag=None, sent=None, taken=None):
        self.buf, self.sems = buf, sems
        self.rank, self.size, self.place = rank, size, place
        self.takes, self.flag = takes, flag
        self.sent = size - 1 if sent is None else sent
        self.taken = size - 1 if taken is None else taken

    def copy(self, src, dst, peer):
        return pltpu.make_async_remote_copy(
            src_ref=src, dst_ref=dst, send_sem=self.sems.at[0], recv_sem=self.sems.at[1],
            device_id=self.place(peer), device_id_type=MESH,
        )

    def start(self, source=None):
        own = self.buf.at[self.rank]
        for k in range(1, self.size):
            peer = lax.rem(self.rank + k, self.size)

            def act(peer=peer):
                self.copy(own if source is None else source.at[peer], own, peer).start()

            if self.takes is None:
                act()
            else:
                pl.when(self.takes(peer))(act)

    def all_of(self, count, act):
        def some(n):
            if n:
                slots = self.buf.at[pl.ds(0, n)]
                act(self.copy(slots, slots, lax.rem(self.rank + 1, self.size)))

        if isinstance(count, tuple):
            pl.when(self.flag)(lambda: some(count[0]))
            pl.when(jnp.logical_not(self.flag))(lambda: some(count[1]))
        else:
            some(count)

    def drain(self):
        self.all_of(self.sent, lambda copy: copy.wait_send())

    def wait(self):
        self.all_of(self.taken, lambda copy: copy.wait_recv())

    def total(self, low=0, high=None):
        out = self.buf[low]
        for i in range(low + 1, self.size if high is None else high):
            out = out + self.buf[i]
        return out


def kernel(
    unit_split, day_split,
    pre_hbm, post_hbm, x_hbm, cohort_hbm, unit_logit_hbm, time_logit_hbm,
    unit_out, time_out,
    pre_ref, post_ref, cohort_ref, unit_logit_ref, time_logit_ref,
    x_buf, high_buf, low_buf, high_turned, low_turned, left_buf, acc_buf, raised_buf, control_buf, moved_buf,
    stat_buf, ux_buf, uz_buf, grad,
    upart, urs, uzh, uag, tpart, trs, tzh, tag, lrs, lzh, utot, uall, ttot,
    in_sem, x_sem, stat_sem, ux_sem, uz_sem, grad_sem,
    urs_sem, uzh_sem, uag_sem, trs_sem, tzh_sem, tag_sem, lrs_sem, lzh_sem, utot_sem, uall_sem, ttot_sem,
):
    nx, nz = unit_split
    ny, nh, nc = day_split
    unit_n, day_n, shards = nx * nz, ny * nh * nc, ny * nc
    units, days = x_buf.shape
    groups = unit_logit_ref.shape[0]
    shard = units // shards
    own_units = units // (shards // 2)
    all_count = day_n * days
    early_ranks, early_days = shards // 2, day_n // 2

    u, d = lax.axis_index("unit"), lax.axis_index("day")
    ux, uz = lax.div(u, nz), lax.rem(u, nz)
    dy, dh, dc = lax.div(d, nh * nc), lax.rem(lax.div(d, nc), nh), lax.rem(d, nc)
    j = dy * nc + dc
    early = j < early_ranks

    def in_shards(rank):
        return {"day": lax.div(rank, nc) * (nh * nc) + dh * nc + lax.rem(rank, nc)}

    def in_high(rank):
        return {"day": dy * (nh * nc) + rank * nc + dc}

    on_unit = lambda rank: {"unit": rank}
    on_day = lambda rank: {"day": rank}
    on_x = lambda rank: {"unit": rank * nz + uz}
    on_z = lambda rank: {"unit": ux * nz + rank}

    barrier = pltpu.get_barrier_semaphore()
    for k in range(1, unit_n):
        pl.semaphore_signal(barrier, inc=1, device_id=on_unit(lax.rem(u + k, unit_n)), device_id_type=MESH)
    for k in range(1, shards):
        pl.semaphore_signal(barrier, inc=1, device_id=in_shards(lax.rem(j + k, shards)), device_id_type=MESH)
    for k in range(1, nh):
        for i in range(early_ranks):
            peer = lax.rem(dh + k, nh) * nc + i // nc * nh * nc + i % nc

            @pl.when(early)
            def _(peer=peer):
                pl.semaphore_signal(barrier, inc=1, device_id=on_day(peer), device_id_type=MESH)

        @pl.when(jnp.logical_not(early))
        def _(k=k):
            pl.semaphore_signal(barrier, inc=1, device_id=in_high(lax.rem(dh + k, nh)), device_id_type=MESH)

    inputs = [
        pltpu.make_async_copy(src, dst, in_sem.at[k])
        for k, (src, dst) in enumerate((
            (unit_logit_hbm, unit_logit_ref), (cohort_hbm, cohort_ref), (time_logit_hbm, time_logit_ref),
            (pre_hbm, pre_ref), (post_hbm, post_ref),
        ))
    ]
    part = units // PARTS
    loads = [
        pltpu.make_async_copy(x_hbm.at[pl.ds(k * part, part)], x_buf.at[pl.ds(k * part, part)], x_sem.at[k])
        for k in range(PARTS)
    ]
    for copy in inputs + loads:
        copy.start()

    stats = Exchange(stat_buf, stat_sem, u, unit_n, on_unit)
    sum_x = Exchange(ux_buf, ux_sem, ux, nx, on_x)
    sum_z = Exchange(uz_buf, uz_sem, uz, nz, on_z)
    to_early = (early_ranks - 1, early_ranks)
    from_early = dict(flag=early, taken=to_early)
    unit_rs = Exchange(urs, urs_sem, j, early_ranks, in_shards)
    unit_zh = Exchange(uzh, uzh_sem, dh, nh, in_high)
    unit_ag = Exchange(uag, uag_sem, j, shards, in_shards, **from_early)
    unit_tot = Exchange(utot, utot_sem, u, unit_n, on_unit)
    unit_all = Exchange(uall, uall_sem, j, shards, in_shards, **from_early)
    time_rs = Exchange(trs, trs_sem, j, shards, in_shards)
    time_zh = Exchange(tzh, tzh_sem, dh, nh, in_high)
    time_ag = Exchange(
        tag, tag_sem, j, shards, in_shards, takes=lambda rank: rank < early_ranks, flag=early, sent=to_early
    )
    lam_rs = Exchange(lrs, lrs_sem, j, shards, in_shards, **from_early)
    lam_zh = Exchange(lzh, lzh_sem, dh, nh, in_high)
    time_grad = Exchange(grad, grad_sem, u, unit_n, on_unit)
    time_tot = Exchange(ttot, ttot_sem, d, early_days, on_day)

    for copy in inputs:
        copy.wait()

    labels = lax.broadcasted_iota(jnp.int32, (groups, units), 0)
    cohort = jnp.broadcast_to(cohort_ref[...], (groups, units))
    treated = jnp.where(cohort == labels, 1.0, 0.0)
    control = jnp.where(cohort > labels, 1.0, 0.0)
    raised = jnp.exp(unit_logit_ref[...]) * control
    for i in range(shards):
        control_buf[i] = control[:, i * shard:(i + 1) * shard]
    for i in range(early_ranks):
        raised_buf[i] = raised[:, i * own_units:(i + 1) * own_units]
    raised_high, raised_low = halves(raised)
    left_buf[...] = jnp.concatenate(
        [raised_high, raised_low, treated, jnp.zeros_like(treated)], axis=0
    ).astype(bf16)
    norm_part = jnp.sum(raised, axis=1, keepdims=True)
    treat_part = jnp.sum(treated, axis=1, keepdims=True)
    ctrl_part = jnp.sum(control, axis=1, keepdims=True)
    rows3 = [to_row(norm_part), to_row(treat_part), to_row(ctrl_part)]
    stat_buf[u] = jnp.concatenate(rows3 + [jnp.zeros((groups - 3, LANES), f32)], axis=0)

    pre_end, post_start = column(pre_ref, groups), column(post_ref, groups)
    before_len = pre_end.astype(f32)
    after_len = (all_count - post_start).astype(f32)
    day_index = d * days + lax.broadcasted_iota(jnp.int32, (groups, days), 1)
    before = jnp.where(day_index < pre_end, 1.0, 0.0)
    after = jnp.where(day_index >= post_start, 1.0, 0.0)
    time_raised = jnp.exp(time_logit_ref[...]) * before
    moved_buf[...] = time_raised
    time_left = jnp.concatenate(halves(time_raised + after), axis=0).astype(bf16)
    scale = jnp.broadcast_to(jnp.where(early, 1.0, 1.0 / after_len), (groups, shard))
    lrs[j] = to_row(jnp.sum(time_raised, axis=1, keepdims=True))

    def split(k):
        rows = pl.ds(k * part, part)
        whole = x_buf[rows, :]
        high = whole.astype(bf16)
        high_buf[rows, :] = high
        low_buf[rows, :] = (whole - high.astype(f32)).astype(bf16)

    def weigh_units(k):
        for i in range(k * part // shard, (k + 1) * part // shard):
            rows = pl.ds(i * shard, shard)
            out = dot_nt(time_left, high_buf[rows, :]) + dot_nt(time_left, low_buf[rows, :])
            tpart[i] = (out[0:groups] + out[groups:]) * scale

    def weigh_rows(k):
        rows = pl.ds(k * part, part)
        left = left_buf[:, k * part:(k + 1) * part]
        return dot_nn(left, high_buf[rows, :]) + dot_nn(left, low_buf[rows, :])

    for k in range(PARTS):
        loads[k].wait()
        split(k)

        @pl.when(early)
        def _(k=k):
            acc = weigh_rows(k)
            if k:
                acc_buf[...] += acc
            else:
                acc_buf[...] = acc

    @pl.when(early)
    def _():
        ux_buf[ux, :, 0:days] = acc_buf[0:groups] + acc_buf[groups:2 * groups]
        ux_buf[ux, :, days:] = acc_buf[2 * groups:3 * groups]

    for k in range(PARTS // 2):
        weigh_units(k)

    pl.semaphore_wait(
        barrier, unit_n - 1 + shards - 1 + jnp.where(early, (nh - 1) * early_ranks, nh - 1)
    )
    @pl.when(early)
    def _():
        sum_x.start()

    for k in range(PARTS // 2, PARTS):
        weigh_units(k)
    trs[j] = tpart[j]
    time_rs.start(tpart)

    @pl.when(early)
    def _():
        lam_rs.start()

    stats.start()

    @pl.when(early)
    def _():
        for k in range(units // CHUNK):
            rows = pl.ds(k * CHUNK, CHUNK)
            high_turned[:, k * CHUNK:(k + 1) * CHUNK] = high_buf[rows, :].T
            low_turned[:, k * CHUNK:(k + 1) * CHUNK] = low_buf[rows, :].T
        sum_x.wait()
        uz_buf[uz] = sum_x.total()
        sum_z.start()

    time_rs.wait()
    tzh[dh, 0] = time_rs.total(0, early_ranks)
    tzh[dh, 1] = time_rs.total(early_ranks, shards)
    time_zh.start()
    lam_rs.wait()
    lzh[dh] = lam_rs.total(0, early_ranks)
    lam_zh.start()

    stats.wait()
    all_stats = stats.total()
    unit_norm = to_col(all_stats[0:1], groups)
    treat_count = jnp.maximum(to_col(all_stats[1:2], groups), 1.0)
    ctrl_count = to_col(all_stats[2:3], groups)

    @pl.when(early)
    def _():
        sum_z.wait()
        sums = sum_z.total()
        residual = (sums[:, 0:days] / unit_norm - sums[:, days:] / treat_count) * before
        res_left = jnp.concatenate(halves(residual), axis=0).astype(bf16)
        for i in range(early_ranks):
            cols = slice(i * own_units, (i + 1) * own_units)
            out = dot_nn(res_left, high_turned[:, cols]) + dot_nn(res_left, low_turned[:, cols])
            upart[i] = out[0:groups] + out[groups:]
        urs[j] = upart[j]
        unit_rs.start(upart)

    time_zh.wait()
    lam_zh.wait()
    lam_sum = to_col(lam_zh.total(), groups)
    both = time_zh.total()
    tag[j] = (both[0] / lam_sum - both[1]) * control_buf[j]
    time_ag.start()

    @pl.when(early)
    def _():
        unit_rs.wait()
        uzh[dh] = unit_rs.total()
        unit_zh.start()

        time_ag.wait()
        for i in range(shards):
            left_buf[0:2 * groups, i * shard:(i + 1) * shard] = jnp.concatenate(
                halves(tag[i]), axis=0
            ).astype(bf16)
        left = left_buf[0:2 * groups, :]
        acc = dot_nn(left, high_buf[...]) + dot_nn(left, low_buf[...])
        grad[u] = acc[0:groups] + acc[groups:]
        time_grad.start()

    @pl.when(early)
    def _():
        unit_zh.wait()
        updated = raised_buf[j] / unit_norm * jnp.exp(-step_rate * unit_zh.total() / jnp.sqrt(before_len))
        uag[j] = updated
        utot[u] = to_row(jnp.sum(updated, axis=1, keepdims=True))
        unit_tot.start()
        unit_ag.start()

        time_grad.wait()
        ctrl_root = jnp.sqrt(jnp.maximum(ctrl_count, 1.0))
        moved = moved_buf[...] / lam_sum * jnp.exp(-step_rate * time_grad.total() / ctrl_root)
        moved_buf[...] = moved
        ttot[d] = to_row(jnp.sum(moved, axis=1, keepdims=True))
        time_tot.start()

        unit_tot.wait()
        uall[j] = unit_tot.total()
        unit_all.start()

    unit_ag.wait()
    unit_all.wait()
    unit_total = jnp.broadcast_to(to_col(unit_all.total(0, early_ranks), groups), (groups, own_units))
    count = jnp.broadcast_to(ctrl_count, (groups, own_units))
    for i in range(early_ranks):
        unit_out[:, i * own_units:(i + 1) * own_units] = uag[i] / unit_total * count

    @pl.when(early)
    def _():
        time_tot.wait()
        time_out[...] = moved_buf[...] / to_col(time_tot.total(), groups) * before_len

    @pl.when(jnp.logical_not(early))
    def _():
        time_out[...] = jnp.zeros_like(time_out)

    for group in (time_rs, stats, time_zh, lam_zh, time_ag):
        group.drain()

    @pl.when(early)
    def _():
        for group in (lam_rs, sum_x, sum_z, unit_rs, unit_zh, unit_tot, unit_ag, unit_all, time_grad, time_tot):
            group.drain()


def local(unit_split, day_split, outcomes, cohort, pre_end, post_start, unit_logit, time_logit):
    groups = pre_end.shape[0]
    units, days = outcomes.shape
    nx, nz = unit_split
    ny, nh, nc = day_split
    unit_n, day_n, shards = nx * nz, ny * nh * nc, ny * nc
    shard = units // shards
    own = shards // 2
    hbm = pl.BlockSpec(memory_space=pl.ANY)
    vmem = pl.BlockSpec(memory_space=pltpu.VMEM)
    dma = lambda n: pltpu.SemaphoreType.DMA((n,))
    slots = lambda n, size: pltpu.VMEM((n, groups, size), f32)
    rows = lambda n: pltpu.VMEM((n, 1, LANES), f32)
    return pl.pallas_call(
        functools.partial(kernel, unit_split, day_split),
        out_shape=(pltpu.VMEM((groups, units), f32), pltpu.VMEM((groups, days), f32)),
        in_specs=[hbm] * 6,
        out_specs=(vmem, vmem),
        scratch_shapes=[
            pltpu.SMEM((groups,), jnp.int32),
            pltpu.SMEM((groups,), jnp.int32),
            pltpu.VMEM((1, units), jnp.int32),
            pltpu.VMEM((groups, units), f32),
            pltpu.VMEM((groups, days), f32),
            pltpu.VMEM((units, days), f32),
            pltpu.VMEM((units, days), bf16),
            pltpu.VMEM((units, days), bf16),
            pltpu.VMEM((days, units), bf16),
            pltpu.VMEM((days, units), bf16),
            pltpu.VMEM((4 * groups, units), bf16),
            pltpu.VMEM((4 * groups, days), f32),
            slots(own, units // own), slots(shards, shard),
            pltpu.VMEM((groups, days), f32),
            slots(unit_n, LANES), slots(nx, 2 * days), slots(nz, 2 * days), slots(unit_n, days),
            slots(own, units // own), slots(own, units // own), slots(nh, units // own), slots(shards, units // own),
            slots(shards, shard), slots(shards, shard),
            pltpu.VMEM((nh, 2, groups, shard), f32),
            slots(shards, shard),
            rows(shards), rows(nh), rows(unit_n), rows(shards), rows(day_n // 2),
            dma(5),
            dma(PARTS),
            *[dma(2)] * 15,
        ],
        compiler_params=pltpu.CompilerParams(collective_id=0, has_side_effects=True),
    )(pre_end, post_start, outcomes, cohort.reshape(1, units), unit_logit, time_logit)


def solution(mesh):
    return jax.shard_map(
        functools.partial(local, UNIT_SPLIT, DAY_SPLIT),
        mesh=mesh,
        in_specs=(P("unit", "day"), P("unit"), P(), P(), P(None, "unit"), P(None, "day")),
        out_specs=(P(None, "unit"), P(None, "day")),
        check_vma=False,
    )
```

```python
import functools

import jax
import jax.numpy as jnp
from jax import lax
from jax.experimental import pallas as pl
from jax.experimental.pallas import tpu as pltpu
from jax.sharding import PartitionSpec as P

MESH = pl.DeviceIdType.MESH
step_rate = 16.0
CHUNK = 256
PARTS = 4
LANES = 128
UNIT_SPLIT = (4, 4)
DAY_SPLIT = (4, 2, 2)
f32, bf16 = jnp.float32, jnp.bfloat16


def dot_nn(a, b):
    return jnp.dot(a, b, preferred_element_type=f32)


def dot_nt(a, b):
    return lax.dot_general(a, b, (((1,), (1,)), ((), ())), preferred_element_type=f32)


def halves(v):
    high = v.astype(bf16).astype(f32)
    return high, v - high


def to_row(col):
    groups = col.shape[0]
    row_id = lax.broadcasted_iota(jnp.int32, (groups, LANES), 0)
    lane_id = lax.broadcasted_iota(jnp.int32, (groups, LANES), 1)
    return jnp.sum(jnp.where(row_id == lane_id, col, 0.0), axis=0, keepdims=True)


def to_col(row, groups):
    row_id = lax.broadcasted_iota(jnp.int32, (groups, LANES), 0)
    lane_id = lax.broadcasted_iota(jnp.int32, (groups, LANES), 1)
    return jnp.sum(jnp.where(row_id == lane_id, row, 0.0), axis=1, keepdims=True)


def column(ref, groups):
    row_id = lax.broadcasted_iota(jnp.int32, (groups, 1), 0)
    out = jnp.zeros((groups, 1), jnp.int32)
    for g in range(groups):
        out = jnp.where(row_id == g, ref[g], out)
    return out


class Exchange:
    def __init__(self, buf, sems, rank, size, place, takes=None, flag=None, sent=None, taken=None):
        self.buf, self.sems = buf, sems
        self.rank, self.size, self.place = rank, size, place
        self.takes, self.flag = takes, flag
        self.sent = size - 1 if sent is None else sent
        self.taken = size - 1 if taken is None else taken

    def copy(self, src, dst, peer):
        return pltpu.make_async_remote_copy(
            src_ref=src, dst_ref=dst, send_sem=self.sems.at[0], recv_sem=self.sems.at[1],
            device_id=self.place(peer), device_id_type=MESH,
        )

    def start(self, source=None):
        own = self.buf.at[self.rank]
        for k in range(1, self.size):
            peer = lax.rem(self.rank + k, self.size)

            def act(peer=peer):
                self.copy(own if source is None else source.at[peer], own, peer).start()

            if self.takes is None:
                act()
            else:
                pl.when(self.takes(peer))(act)

    def all_of(self, count, act):
        def some(n):
            if n:
                slots = self.buf.at[pl.ds(0, n)]
                act(self.copy(slots, slots, lax.rem(self.rank + 1, self.size)))

        if isinstance(count, tuple):
            pl.when(self.flag)(lambda: some(count[0]))
            pl.when(jnp.logical_not(self.flag))(lambda: some(count[1]))
        else:
            some(count)

    def drain(self):
        self.all_of(self.sent, lambda copy: copy.wait_send())

    def wait(self):
        self.all_of(self.taken, lambda copy: copy.wait_recv())

    def total(self, low=0, high=None):
        out = self.buf[low]
        for i in range(low + 1, self.size if high is None else high):
            out = out + self.buf[i]
        return out


class Total:
    def copy(self, own, place):
        return pltpu.make_async_remote_copy(
            src_ref=own, dst_ref=own, send_sem=self.sems.at[0], recv_sem=self.sems.at[1],
            device_id=place, device_id_type=MESH,
        )

    def some(self, n):
        slots = self.buf.at[pl.ds(0, n)]
        return self.copy(slots, self.any_peer)

    def wait(self):
        self.some(self.members - 1).wait_recv()

    def total(self):
        out = self.buf[0]
        for i in range(1, self.members):
            out = out + self.buf[i]
        return out


class RingTotal(Total):
    def __init__(self, buf, sems, ux, uz, nx, nz, steps, on_ring):
        self.buf, self.sems, self.members = buf, sems, nx * nz
        self.ux, self.own, self.nx, self.steps, self.on_ring = ux, ux * nz + uz, nx, steps, on_ring
        self.any_peer = on_ring(ux, 1)

    def start(self):
        own = self.buf.at[self.own]
        for step in (0,) + self.steps:
            for k in range(0 if step else 1, self.nx):
                self.copy(own, self.on_ring(lax.rem(self.ux + k, self.nx), -step)).start()

    def drain(self):
        self.some(self.members - 1).wait_send()


class DayTotal(Total):
    def __init__(self, buf, sems, ux, uz, dy, dh, dc, nz, ny, nh, nc, at):
        self.buf, self.sems, self.members = buf, sems, ny * nh * nc
        self.ux, self.uz, self.dy, self.dh, self.dc, self.nz, self.ny, self.nh, self.nc, self.at = (
            ux, uz, dy, dh, dc, nz, ny, nh, nc, at
        )
        self.own = dy * (nh * nc) + dh * nc + dc
        self.rank, self.ranks = dy * nc + dc, ny * nc
        self.any_peer = at(ux, uz, dy, 1 - dh, dc)

    def start(self):
        own = self.buf.at[self.own]
        for k in range(1, self.ranks):
            peer = lax.rem(self.rank + k, self.ranks)
            self.copy(own, self.at(self.ux, self.uz, lax.div(peer, self.nc), self.dh, lax.rem(peer, self.nc))).start()
        for end, firsts in ((self.nz - 1, range(self.nz // 2)), (0, range(self.nz // 2, self.nz))):

            @pl.when(self.uz == end)
            def _(firsts=firsts):
                for q in firsts:
                    for k in range(self.ranks):
                        self.copy(own, self.at(self.ux, q, k // self.nc, 1 - self.dh, k % self.nc)).start()

    def drain(self):
        self.some(self.ranks - 1).wait_send()

        @pl.when((self.uz == 0) | (self.uz == self.nz - 1))
        def _():
            self.some(self.nz // 2 * self.ranks).wait_send()


def kernel(
    unit_split, day_split,
    pre_hbm, post_hbm, x_hbm, cohort_hbm, unit_logit_hbm, time_logit_hbm,
    unit_out, time_out,
    pre_ref, post_ref, cohort_ref, unit_logit_ref, time_logit_ref,
    x_buf, high_buf, low_buf, high_turned, low_turned, left_buf, raised_buf, control_buf, moved_buf,
    stat_buf, ux_buf, uz_buf, grad,
    upart, urs, uzh, uag, tpart, trs, tzh, tag, lrs, lzh, utot, uall, ttot,
    in_sem, x_sem, stat_sem, ux_sem, uz_sem, grad_sem,
    urs_sem, uzh_sem, uag_sem, trs_sem, tzh_sem, tag_sem, lrs_sem, lzh_sem, utot_sem, uall_sem, ttot_sem,
):
    nx, nz = unit_split
    ny, nh, nc = day_split
    unit_n, day_n, shards = nx * nz, ny * nh * nc, ny * nc
    units, days = x_buf.shape
    groups = unit_logit_ref.shape[0]
    shard = units // shards
    own_units = units // (shards // 2)
    all_count = day_n * days
    early_ranks = shards // 2

    u, d = lax.axis_index("unit"), lax.axis_index("day")
    ux, uz = lax.div(u, nz), lax.rem(u, nz)
    dy, dh, dc = lax.div(d, nh * nc), lax.rem(lax.div(d, nc), nh), lax.rem(d, nc)
    j = dy * nc + dc
    early = j < early_ranks

    def in_shards(rank):
        return {"day": lax.div(rank, nc) * (nh * nc) + dh * nc + lax.rem(rank, nc)}

    def in_high(rank):
        return {"day": dy * (nh * nc) + rank * nc + dc}

    def at(x, z, y, h, c):
        return {"unit": x * nz + z, "day": y * (nh * nc) + h * nc + c}

    ring = nh * nz
    ring_steps = tuple(k for k in range(-(nz // 2) + 1, nz // 2 + 1) if k)

    def on_ring(x, step):
        z = lax.rem(dh * nz + uz + step + ring, ring)
        return at(x, lax.rem(z, nz), dy, lax.div(z, nz), dc)

    on_unit = lambda rank: {"unit": rank}
    on_x = lambda rank: {"unit": rank * nz + uz}
    on_z = lambda rank: {"unit": ux * nz + rank}

    inputs = [
        pltpu.make_async_copy(src, dst, in_sem.at[k])
        for k, (src, dst) in enumerate((
            (time_logit_hbm, time_logit_ref), (pre_hbm, pre_ref), (post_hbm, post_ref),
            (unit_logit_hbm, unit_logit_ref), (cohort_hbm, cohort_ref),
        ))
    ]
    part = units // PARTS
    loads = [
        pltpu.make_async_copy(x_hbm.at[pl.ds(k * part, part)], x_buf.at[pl.ds(k * part, part)], x_sem.at[k])
        for k in range(PARTS)
    ]
    for copy in inputs + loads:
        copy.start()

    barrier = pltpu.get_barrier_semaphore()

    def greet(place):
        pl.semaphore_signal(barrier, inc=1, device_id=place, device_id_type=MESH)

    for k in range(1, unit_n):
        greet(on_unit(lax.rem(u + k, unit_n)))
    for k in range(1, shards):
        greet(in_shards(lax.rem(j + k, shards)))

    @pl.when(early)
    def _():
        for k in range(1, nh):
            for i in range(early_ranks):
                for q in range(nz):
                    greet(at(ux, q, i // nc, lax.rem(dh + k, nh), i % nc))
        for step in ring_steps:
            for k in range(nx):
                greet(on_ring(k, step))
                greet(on_ring(k, -step))

    @pl.when(jnp.logical_not(early))
    def _():
        for k in range(1, nh):
            greet(in_high(lax.rem(dh + k, nh)))

    stats = Exchange(stat_buf, stat_sem, u, unit_n, on_unit)
    sum_x = Exchange(ux_buf, ux_sem, ux, nx, on_x)
    sum_z = Exchange(uz_buf, uz_sem, uz, nz, on_z)
    to_early = (early_ranks - 1, early_ranks)
    from_early = dict(flag=early, taken=to_early)
    unit_rs = Exchange(urs, urs_sem, j, early_ranks, in_shards)
    unit_zh = Exchange(uzh, uzh_sem, dh, nh, in_high)
    unit_ag = Exchange(uag, uag_sem, j, shards, in_shards, **from_early)
    unit_tot = RingTotal(utot, utot_sem, ux, uz, nx, nz, ring_steps, on_ring)
    unit_all = Exchange(uall, uall_sem, j, shards, in_shards, **from_early)
    time_rs = Exchange(trs, trs_sem, j, shards, in_shards)
    time_zh = Exchange(tzh, tzh_sem, dh, nh, in_high)
    time_ag = Exchange(
        tag, tag_sem, j, shards, in_shards, takes=lambda rank: rank < early_ranks, flag=early, sent=to_early
    )
    lam_rs = Exchange(lrs, lrs_sem, j, shards, in_shards, **from_early)
    lam_zh = Exchange(lzh, lzh_sem, dh, nh, in_high)
    time_grad = Exchange(grad, grad_sem, u, unit_n, on_unit)
    time_tot = DayTotal(ttot, ttot_sem, ux, uz, dy, dh, dc, nz, ny // 2, nh, nc, at)

    for copy in inputs[:3]:
        copy.wait()
    pre_end, post_start = column(pre_ref, groups), column(post_ref, groups)
    before_len = pre_end.astype(f32)
    after_len = (all_count - post_start).astype(f32)
    day_index = d * days + lax.broadcasted_iota(jnp.int32, (groups, days), 1)
    before = jnp.where(day_index < pre_end, 1.0, 0.0)
    after = jnp.where(day_index >= post_start, 1.0, 0.0)
    time_raised = jnp.exp(time_logit_ref[...]) * before
    moved_buf[...] = time_raised
    time_left = jnp.concatenate(halves(time_raised + after), axis=0).astype(bf16)
    scale = jnp.broadcast_to(jnp.where(early, 1.0, 1.0 / after_len), (groups, shard))
    lrs[j] = to_row(jnp.sum(time_raised, axis=1, keepdims=True))

    def split(k):
        rows = pl.ds(k * part, part)
        whole = x_buf[rows, :]
        high = whole.astype(bf16)
        high_buf[rows, :] = high
        low_buf[rows, :] = (whole - high.astype(f32)).astype(bf16)

    def weigh_units(k):
        for i in range(k * part // shard, (k + 1) * part // shard):
            rows = pl.ds(i * shard, shard)
            out = dot_nt(time_left, high_buf[rows, :]) + dot_nt(time_left, low_buf[rows, :])
            tpart[i] = (out[0:groups] + out[groups:]) * scale

    def local_weights():
        for copy in inputs[3:]:
            copy.wait()

        labels = lax.broadcasted_iota(jnp.int32, (groups, units), 0)
        cohort = jnp.broadcast_to(cohort_ref[...], (groups, units))
        treated = jnp.where(cohort == labels, 1.0, 0.0)
        control = jnp.where(cohort > labels, 1.0, 0.0)
        raised = jnp.exp(unit_logit_ref[...]) * control
        for i in range(shards):
            control_buf[i] = control[:, i * shard:(i + 1) * shard]
        for i in range(early_ranks):
            raised_buf[i] = raised[:, i * own_units:(i + 1) * own_units]
        raised_high, raised_low = halves(raised)
        left_buf[...] = jnp.concatenate(
            [raised_high, raised_low, treated, jnp.zeros_like(treated)], axis=0
        ).astype(bf16)
        norm_part = jnp.sum(raised, axis=1, keepdims=True)
        treat_part = jnp.sum(treated, axis=1, keepdims=True)
        ctrl_part = jnp.sum(control, axis=1, keepdims=True)
        rows3 = [to_row(norm_part), to_row(treat_part), to_row(ctrl_part)]
        stat_buf[u] = jnp.concatenate(rows3 + [jnp.zeros((groups - 3, LANES), f32)], axis=0)

    def weigh_rows(k):
        rows = pl.ds(k * part, part)
        left = left_buf[:, k * part:(k + 1) * part]
        acc = dot_nn(left, high_buf[rows, :]) + dot_nn(left, low_buf[rows, :])
        fit, treat = acc[0:groups] + acc[groups:2 * groups], acc[2 * groups:3 * groups]
        if k:
            fit, treat = fit + own_sums[:, 0:days], treat + own_sums[:, days:]
        own_sums[:, 0:days] = fit
        own_sums[:, days:] = treat

    own_sums = ux_buf.at[ux]

    @pl.when(early)
    def _():
        local_weights()
        for k in range(PARTS):
            loads[k].wait()
            if k:
                weigh_rows(k - 1)
            split(k)
        weigh_rows(PARTS - 1)
        weigh_units(0)

    @pl.when(jnp.logical_not(early))
    def _():
        for k in range(PARTS):
            loads[k].wait()
            if k:
                weigh_units(k - 1)
            split(k)
        weigh_units(PARTS - 1)

    pl.semaphore_wait(
        barrier,
        unit_n - 1 + shards - 1
        + jnp.where(early, (nh - 1) * early_ranks * nz + 2 * len(ring_steps) * nx, nh - 1),
    )
    @pl.when(early)
    def _():
        sum_x.start()
        for k in range(1, PARTS):
            weigh_units(k)

    trs[j] = tpart[j]
    time_rs.start(tpart)

    @pl.when(early)
    def _():
        lam_rs.start()

    pl.when(jnp.logical_not(early))(local_weights)
    stats.start()

    @pl.when(early)
    def _():
        for k in range(units // CHUNK):
            rows = pl.ds(k * CHUNK, CHUNK)
            high_turned[:, k * CHUNK:(k + 1) * CHUNK] = high_buf[rows, :].T
            low_turned[:, k * CHUNK:(k + 1) * CHUNK] = low_buf[rows, :].T

    @pl.when(early)
    def _():
        sum_x.wait()
        uz_buf[uz] = sum_x.total()
        sum_z.start()

    time_rs.wait()
    tzh[dh, 0] = time_rs.total(0, early_ranks)
    tzh[dh, 1] = time_rs.total(early_ranks, shards)
    time_zh.start()
    lam_rs.wait()
    lzh[dh] = lam_rs.total(0, early_ranks)
    lam_zh.start()

    stats.wait()
    all_stats = stats.total()
    unit_norm = to_col(all_stats[0:1], groups)
    treat_count = jnp.maximum(to_col(all_stats[1:2], groups), 1.0)
    ctrl_count = to_col(all_stats[2:3], groups)

    @pl.when(early)
    def _():
        sum_z.wait()
        sums = sum_z.total()
        residual = (sums[:, 0:days] / unit_norm - sums[:, days:] / treat_count) * before
        res_left = jnp.concatenate(halves(residual), axis=0).astype(bf16)
        for i in range(early_ranks):
            cols = slice(i * own_units, (i + 1) * own_units)
            out = dot_nn(res_left, high_turned[:, cols]) + dot_nn(res_left, low_turned[:, cols])
            upart[i] = out[0:groups] + out[groups:]
        urs[j] = upart[j]
        unit_rs.start(upart)

    time_zh.wait()
    lam_zh.wait()
    lam_sum = to_col(lam_zh.total(), groups)
    both = time_zh.total()
    tag[j] = (both[0] / lam_sum - both[1]) * control_buf[j]
    time_ag.start()

    @pl.when(early)
    def _():
        unit_rs.wait()
        uzh[dh] = unit_rs.total()
        unit_zh.start()

        time_ag.wait()
        for i in range(shards):
            left_buf[0:2 * groups, i * shard:(i + 1) * shard] = jnp.concatenate(
                halves(tag[i]), axis=0
            ).astype(bf16)
        left = left_buf[0:2 * groups, :]
        acc = dot_nn(left, high_buf[...]) + dot_nn(left, low_buf[...])
        grad[u] = acc[0:groups] + acc[groups:]
        time_grad.start()

    @pl.when(early)
    def _():
        unit_zh.wait()
        updated = raised_buf[j] / unit_norm * jnp.exp(-step_rate * unit_zh.total() / jnp.sqrt(before_len))
        uag[j] = updated
        utot[u] = to_row(jnp.sum(updated, axis=1, keepdims=True))
        unit_tot.start()
        unit_ag.start()

        time_grad.wait()
        ctrl_root = jnp.sqrt(jnp.maximum(ctrl_count, 1.0))
        moved = moved_buf[...] / lam_sum * jnp.exp(-step_rate * time_grad.total() / ctrl_root)
        moved_buf[...] = moved
        ttot[d] = to_row(jnp.sum(moved, axis=1, keepdims=True))
        time_tot.start()

        unit_tot.wait()
        uall[j] = unit_tot.total()
        unit_all.start()

    unit_ag.wait()
    unit_all.wait()
    unit_total = jnp.broadcast_to(to_col(unit_all.total(0, early_ranks), groups), (groups, own_units))
    count = jnp.broadcast_to(ctrl_count, (groups, own_units))
    for i in range(early_ranks):
        unit_out[:, i * own_units:(i + 1) * own_units] = uag[i] / unit_total * count

    @pl.when(early)
    def _():
        time_tot.wait()
        time_out[...] = moved_buf[...] / to_col(time_tot.total(), groups) * before_len

    @pl.when(jnp.logical_not(early))
    def _():
        time_out[...] = jnp.zeros_like(time_out)

    for group in (time_rs, stats, time_zh, lam_zh, time_ag):
        group.drain()

    @pl.when(early)
    def _():
        for group in (lam_rs, sum_x, sum_z, unit_rs, unit_zh, unit_tot, unit_ag, unit_all, time_grad, time_tot):
            group.drain()


def put_out(unit_in, time_in, unit_out, time_out, sems):
    copies = [
        pltpu.make_async_copy(unit_in, unit_out, sems.at[0]),
        pltpu.make_async_copy(time_in, time_out, sems.at[1]),
    ]
    for copy in copies:
        copy.start()
    for copy in copies:
        copy.wait()


def local(unit_split, day_split, outcomes, cohort, pre_end, post_start, unit_logit, time_logit):
    groups = pre_end.shape[0]
    units, days = outcomes.shape
    nx, nz = unit_split
    ny, nh, nc = day_split
    unit_n, day_n, shards = nx * nz, ny * nh * nc, ny * nc
    shard = units // shards
    own = shards // 2
    hbm = pl.BlockSpec(memory_space=pl.ANY)
    vmem = pl.BlockSpec(memory_space=pltpu.VMEM)
    dma = lambda n: pltpu.SemaphoreType.DMA((n,))
    slots = lambda n, size: pltpu.VMEM((n, groups, size), f32)
    rows = lambda n: pltpu.VMEM((n, 1, LANES), f32)
    unit_weights, time_weights = pl.pallas_call(
        functools.partial(kernel, unit_split, day_split),
        out_shape=(pltpu.VMEM((groups, units), f32), pltpu.VMEM((groups, days), f32)),
        in_specs=[hbm] * 6,
        out_specs=(vmem, vmem),
        scratch_shapes=[
            pltpu.SMEM((groups,), jnp.int32),
            pltpu.SMEM((groups,), jnp.int32),
            pltpu.VMEM((1, units), jnp.int32),
            pltpu.VMEM((groups, units), f32),
            pltpu.VMEM((groups, days), f32),
            pltpu.VMEM((units, days), f32),
            pltpu.VMEM((units, days), bf16),
            pltpu.VMEM((units, days), bf16),
            pltpu.VMEM((days, units), bf16),
            pltpu.VMEM((days, units), bf16),
            pltpu.VMEM((4 * groups, units), bf16),
            slots(own, units // own), slots(shards, shard),
            pltpu.VMEM((groups, days), f32),
            slots(unit_n, LANES), slots(nx, 2 * days), slots(nz, 2 * days), slots(unit_n, days),
            slots(own, units // own), slots(own, units // own), slots(nh, units // own), slots(shards, units // own),
            slots(shards, shard), slots(shards, shard),
            pltpu.VMEM((nh, 2, groups, shard), f32),
            slots(shards, shard),
            rows(shards), rows(nh), rows(unit_n), rows(shards), rows(day_n // 2),
            dma(5),
            dma(PARTS),
            *[dma(2)] * 15,
        ],
        compiler_params=pltpu.CompilerParams(collective_id=0, has_side_effects=True),
    )(pre_end, post_start, outcomes, cohort.reshape(1, units), unit_logit, time_logit)
    return pl.pallas_call(
        put_out,
        out_shape=(
            jax.ShapeDtypeStruct((groups, units), f32),
            jax.ShapeDtypeStruct((groups, days), f32),
        ),
        in_specs=[vmem] * 2,
        out_specs=(hbm, hbm),
        scratch_shapes=[dma(2)],
    )(*(pltpu.with_memory_space_constraint(v, pltpu.VMEM) for v in (unit_weights, time_weights)))


def solution(mesh):
    return jax.shard_map(
        functools.partial(local, UNIT_SPLIT, DAY_SPLIT),
        mesh=mesh,
        in_specs=(P("unit", "day"), P("unit"), P(), P(), P(None, "unit"), P(None, "day")),
        out_specs=(P(None, "unit"), P(None, "day")),
        check_vma=False,
    )
```

```python
import functools

import jax
import jax.numpy as jnp
from jax import lax
from jax.experimental import pallas as pl
from jax.experimental.pallas import tpu as pltpu
from jax.sharding import PartitionSpec as P

MESH = pl.DeviceIdType.MESH
step_rate = 16.0
CHUNK = 256
PARTS = 4
LANES = 128
UNIT_SPLIT = (4, 4)
DAY_SPLIT = (4, 2, 2)
f32, bf16 = jnp.float32, jnp.bfloat16


def dot_nn(a, b):
    return jnp.dot(a, b, preferred_element_type=f32)


def dot_nt(a, b):
    return lax.dot_general(a, b, (((1,), (1,)), ((), ())), preferred_element_type=f32)


def halves(v):
    high = v.astype(bf16).astype(f32)
    return high, v - high


def to_row(col, first=0):
    groups = col.shape[0]
    row_id = lax.broadcasted_iota(jnp.int32, (groups, LANES), 0)
    lane_id = lax.broadcasted_iota(jnp.int32, (groups, LANES), 1)
    return jnp.sum(jnp.where(row_id + first == lane_id, col, 0.0), axis=0, keepdims=True)


def to_col(row, groups, first=0):
    row_id = lax.broadcasted_iota(jnp.int32, (groups, LANES), 0)
    lane_id = lax.broadcasted_iota(jnp.int32, (groups, LANES), 1)
    return jnp.sum(jnp.where(row_id + first == lane_id, row, 0.0), axis=1, keepdims=True)


def column(ref, groups):
    row_id = lax.broadcasted_iota(jnp.int32, (groups, 1), 0)
    out = jnp.zeros((groups, 1), jnp.int32)
    for g in range(groups):
        out = jnp.where(row_id == g, ref[g], out)
    return out


class Exchange:
    def __init__(self, buf, sems, rank, size, place, takes=None, flag=None, sent=None, taken=None):
        self.buf, self.sems = buf, sems
        self.rank, self.size, self.place = rank, size, place
        self.takes, self.flag = takes, flag
        self.sent = size - 1 if sent is None else sent
        self.taken = size - 1 if taken is None else taken

    def copy(self, src, dst, peer):
        return pltpu.make_async_remote_copy(
            src_ref=src, dst_ref=dst, send_sem=self.sems.at[0], recv_sem=self.sems.at[1],
            device_id=self.place(peer), device_id_type=MESH,
        )

    def start(self, source=None):
        own = self.buf.at[self.rank]
        for k in range(1, self.size):
            peer = lax.rem(self.rank + k, self.size)

            def act(peer=peer):
                self.copy(own if source is None else source.at[peer], own, peer).start()

            if self.takes is None:
                act()
            else:
                pl.when(self.takes(peer))(act)

    def all_of(self, count, act):
        def some(n):
            if n:
                slots = self.buf.at[pl.ds(0, n)]
                act(self.copy(slots, slots, lax.rem(self.rank + 1, self.size)))

        if isinstance(count, tuple):
            pl.when(self.flag)(lambda: some(count[0]))
            pl.when(jnp.logical_not(self.flag))(lambda: some(count[1]))
        else:
            some(count)

    def drain(self):
        self.all_of(self.sent, lambda copy: copy.wait_send())

    def wait(self):
        self.all_of(self.taken, lambda copy: copy.wait_recv())

    def total(self, low=0, high=None):
        out = self.buf[low]
        for i in range(low + 1, self.size if high is None else high):
            out = out + self.buf[i]
        return out


class Total:
    def copy(self, own, place):
        return pltpu.make_async_remote_copy(
            src_ref=own, dst_ref=own, send_sem=self.sems.at[0], recv_sem=self.sems.at[1],
            device_id=place, device_id_type=MESH,
        )

    def some(self, n):
        slots = self.buf.at[pl.ds(0, n)]
        return self.copy(slots, self.any_peer)

    def wait(self):
        self.some(self.members - 1).wait_recv()

    def total(self):
        out = self.buf[0]
        for i in range(1, self.members):
            out = out + self.buf[i]
        return out


class RingTotal(Total):
    def __init__(self, buf, sems, ux, uz, nx, nz, steps, on_ring):
        self.buf, self.sems, self.members = buf, sems, nx * nz
        self.ux, self.own, self.nx, self.steps, self.on_ring = ux, ux * nz + uz, nx, steps, on_ring
        self.any_peer = on_ring(ux, 1)

    def start(self):
        own = self.buf.at[self.own]
        for step in (0,) + self.steps:
            for k in range(0 if step else 1, self.nx):
                self.copy(own, self.on_ring(lax.rem(self.ux + k, self.nx), -step)).start()

    def drain(self):
        self.some(self.members - 1).wait_send()


class DayTotal(Total):
    def __init__(self, buf, sems, ux, uz, dy, dh, dc, nz, ny, nh, nc, at):
        self.buf, self.sems, self.members = buf, sems, ny * nh * nc
        self.ux, self.uz, self.dy, self.dh, self.dc, self.nz, self.ny, self.nh, self.nc, self.at = (
            ux, uz, dy, dh, dc, nz, ny, nh, nc, at
        )
        self.own = dy * (nh * nc) + dh * nc + dc
        self.rank, self.ranks = dy * nc + dc, ny * nc
        self.any_peer = at(ux, uz, dy, 1 - dh, dc)

    def start(self):
        own = self.buf.at[self.own]
        for k in range(1, self.ranks):
            peer = lax.rem(self.rank + k, self.ranks)
            self.copy(own, self.at(self.ux, self.uz, lax.div(peer, self.nc), self.dh, lax.rem(peer, self.nc))).start()
        for end, firsts in ((self.nz - 1, range(self.nz // 2)), (0, range(self.nz // 2, self.nz))):

            @pl.when(self.uz == end)
            def _(firsts=firsts):
                for q in firsts:
                    for k in range(self.ranks):
                        self.copy(own, self.at(self.ux, q, k // self.nc, 1 - self.dh, k % self.nc)).start()

    def drain(self):
        self.some(self.ranks - 1).wait_send()

        @pl.when((self.uz == 0) | (self.uz == self.nz - 1))
        def _():
            self.some(self.nz // 2 * self.ranks).wait_send()


def kernel(
    unit_split, day_split,
    pre_hbm, post_hbm, x_hbm, cohort_hbm, unit_logit_hbm, time_logit_hbm,
    unit_out, time_out,
    pre_ref, post_ref, cohort_ref, unit_logit_ref, time_logit_ref,
    x_buf, high_buf, low_buf, high_turned, low_turned, left_buf, raised_buf, control_buf, moved_buf,
    stat_buf, ux_buf, uz_buf, grad,
    upart, urs, uzh, uag, tpart, trs, tzh, tag, lrs, lzh, utot, uall, ttot,
    in_sem, x_sem, near_sem, ux_sem, uz_sem, grad_sem,
    urs_sem, uzh_sem, uag_sem, trs_sem, tzh_sem, tag_sem, lrs_sem, lzh_sem, utot_sem, uall_sem, ttot_sem,
):
    nx, nz = unit_split
    ny, nh, nc = day_split
    unit_n, day_n, shards = nx * nz, ny * nh * nc, ny * nc
    units, days = x_buf.shape
    groups = unit_logit_ref.shape[0]
    shard = units // shards
    own_units = units // (shards // 2)
    all_count = day_n * days
    early_ranks = shards // 2

    u, d = lax.axis_index("unit"), lax.axis_index("day")
    ux, uz = lax.div(u, nz), lax.rem(u, nz)
    dy, dh, dc = lax.div(d, nh * nc), lax.rem(lax.div(d, nc), nh), lax.rem(d, nc)
    j = dy * nc + dc
    early = j < early_ranks

    def in_shards(rank):
        return {"day": lax.div(rank, nc) * (nh * nc) + dh * nc + lax.rem(rank, nc)}

    def in_high(rank):
        return {"day": dy * (nh * nc) + rank * nc + dc}

    def at(x, z, y, h, c):
        return {"unit": x * nz + z, "day": y * (nh * nc) + h * nc + c}

    ring = nh * nz
    ring_steps = tuple(k for k in range(-(nz // 2) + 1, nz // 2 + 1) if k)

    def on_ring(x, step):
        z = lax.rem(dh * nz + uz + step + ring, ring)
        return at(x, lax.rem(z, nz), dy, lax.div(z, nz), dc)

    on_unit = lambda rank: {"unit": rank}
    on_x = lambda rank: {"unit": rank * nz + uz}
    on_z = lambda rank: {"unit": ux * nz + rank}

    barrier = pltpu.get_barrier_semaphore()

    def greet(place):
        pl.semaphore_signal(barrier, inc=1, device_id=place, device_id_type=MESH)

    for k in range(1, shards):
        greet(in_shards(lax.rem(j + k, shards)))
    for step in (-2, -1, 1, 2):
        greet(on_ring(ux, step))

    @pl.when(early)
    def _():
        for k in range(1, nx):
            greet(on_x(lax.rem(ux + k, nx)))

    inputs = [
        pltpu.make_async_copy(src, dst, in_sem.at[k])
        for k, (src, dst) in enumerate((
            (time_logit_hbm, time_logit_ref), (pre_hbm, pre_ref), (post_hbm, post_ref),
            (unit_logit_hbm, unit_logit_ref), (cohort_hbm, cohort_ref),
        ))
    ]
    part = units // PARTS
    loads = [
        pltpu.make_async_copy(x_hbm.at[pl.ds(k * part, part)], x_buf.at[pl.ds(k * part, part)], x_sem.at[k])
        for k in range(PARTS)
    ]
    for copy in inputs + loads:
        copy.start()

    sum_x = Exchange(ux_buf, ux_sem, ux, nx, on_x)
    sum_z = Exchange(uz_buf, uz_sem, uz, nz, on_z)
    to_early = (early_ranks - 1, early_ranks)
    from_early = dict(flag=early, taken=to_early)
    unit_rs = Exchange(urs, urs_sem, j, early_ranks, in_shards)
    unit_zh = Exchange(uzh, uzh_sem, dh, nh, in_high)
    unit_ag = Exchange(uag, uag_sem, j, shards, in_shards, **from_early)
    unit_tot = RingTotal(utot, utot_sem, ux, uz, nx, nz, ring_steps, on_ring)
    unit_all = Exchange(uall, uall_sem, j, shards, in_shards, **from_early)
    time_rs = Exchange(trs, trs_sem, j, shards, in_shards)
    time_zh = Exchange(tzh, tzh_sem, dh, nh, in_high)
    time_ag = Exchange(
        tag, tag_sem, j, shards, in_shards, takes=lambda rank: rank < early_ranks, flag=early, sent=to_early
    )
    lam_rs = Exchange(lrs, lrs_sem, j, shards, in_shards, **from_early)
    lam_zh = Exchange(lzh, lzh_sem, dh, nh, in_high)
    time_grad = Exchange(grad, grad_sem, u, unit_n, on_unit)
    time_tot = DayTotal(ttot, ttot_sem, ux, uz, dy, dh, dc, nz, ny // 2, nh, nc, at)

    for copy in inputs[:3]:
        copy.wait()
    pre_end, post_start = column(pre_ref, groups), column(post_ref, groups)
    before_len = pre_end.astype(f32)
    after_len = (all_count - post_start).astype(f32)
    day_index = d * days + lax.broadcasted_iota(jnp.int32, (groups, days), 1)
    before = jnp.where(day_index < pre_end, 1.0, 0.0)
    after = jnp.where(day_index >= post_start, 1.0, 0.0)
    time_raised = jnp.exp(time_logit_ref[...]) * before
    moved_buf[...] = time_raised
    time_left = jnp.concatenate(halves(time_raised + after), axis=0).astype(bf16)
    scale = jnp.broadcast_to(jnp.where(early, 1.0, 1.0 / after_len), (groups, shard))
    lrs[j] = to_row(jnp.sum(time_raised, axis=1, keepdims=True))

    def hear():
        pl.semaphore_wait(near_sem.at[0], 1)
        pl.semaphore_wait(near_sem.at[1], 1)

    def split(k):
        rows = pl.ds(k * part, part)
        whole = x_buf[rows, :]
        high = whole.astype(bf16)
        high_buf[rows, :] = high
        low_buf[rows, :] = (whole - high.astype(f32)).astype(bf16)

    def weigh_units(k):
        for i in range(k * part // shard, (k + 1) * part // shard):
            rows = pl.ds(i * shard, shard)
            out = dot_nt(time_left, high_buf[rows, :]) + dot_nt(time_left, low_buf[rows, :])
            tpart[i] = (out[0:groups] + out[groups:]) * scale

    def local_weights():
        for copy in inputs[3:]:
            copy.wait()

        labels = lax.broadcasted_iota(jnp.int32, (groups, units), 0)
        cohort = jnp.broadcast_to(cohort_ref[...], (groups, units))
        treated = jnp.where(cohort == labels, 1.0, 0.0)
        control = jnp.where(cohort > labels, 1.0, 0.0)
        raised = jnp.exp(unit_logit_ref[...]) * control
        for i in range(shards):
            control_buf[i] = control[:, i * shard:(i + 1) * shard]
        for i in range(early_ranks):
            raised_buf[i] = raised[:, i * own_units:(i + 1) * own_units]
        raised_high, raised_low = halves(raised)
        left_buf[...] = jnp.concatenate(
            [raised_high, raised_low, treated, jnp.zeros_like(treated)], axis=0
        ).astype(bf16)
        norm_part = jnp.sum(raised, axis=1, keepdims=True)
        treat_part = jnp.sum(treated, axis=1, keepdims=True)
        ctrl_part = jnp.sum(control, axis=1, keepdims=True)
        lane = lax.broadcasted_iota(jnp.int32, (groups, LANES), 1)
        ux_buf[ux, :, 2 * days:] = jnp.where(
            lane == 0, norm_part, jnp.where(lane == 1, treat_part, jnp.where(lane == 2, ctrl_part, 0.0))
        )

    def weigh_rows(k):
        rows = pl.ds(k * part, part)
        left = left_buf[:, k * part:(k + 1) * part]
        acc = dot_nn(left, high_buf[rows, :]) + dot_nn(left, low_buf[rows, :])
        fit, treat = acc[0:groups] + acc[groups:2 * groups], acc[2 * groups:3 * groups]
        if k:
            fit, treat = fit + own_sums[:, 0:days], treat + own_sums[:, days:2 * days]
        own_sums[:, 0:days] = fit
        own_sums[:, days:2 * days] = treat

    own_sums = ux_buf.at[ux]

    def turn(k):
        for i in range(k * part // CHUNK, (k + 1) * part // CHUNK):
            rows = pl.ds(i * CHUNK, CHUNK)
            high_turned[:, i * CHUNK:(i + 1) * CHUNK] = high_buf[rows, :].T
            low_turned[:, i * CHUNK:(i + 1) * CHUNK] = low_buf[rows, :].T

    def weigh_turned(i):
        cols = slice(i * shard, (i + 1) * shard)
        out = dot_nn(time_left, high_turned[:, cols]) + dot_nn(time_left, low_turned[:, cols])
        tpart[i] = (out[0:groups] + out[groups:]) * scale

    @pl.when(early)
    def _():
        local_weights()
        for k in range(PARTS):
            loads[k].wait()
            if k:
                turn(k - 1)
                weigh_rows(k - 1)
            split(k)
        turn(PARTS - 1)
        weigh_rows(PARTS - 1)
        for i in range(shards // 2):
            weigh_turned(i)

    @pl.when(jnp.logical_not(early))
    def _():
        for k in range(PARTS):
            loads[k].wait()
            if k:
                weigh_units(k - 1)
            split(k)
        weigh_units(PARTS - 1)

    pl.semaphore_wait(barrier, shards - 1 + 4 + jnp.where(early, nx - 1, 0))
    pl.semaphore_signal(near_sem.at[0], inc=1, device_id=on_ring(ux, 2), device_id_type=MESH)
    pl.semaphore_signal(near_sem.at[1], inc=1, device_id=on_ring(ux, -2), device_id_type=MESH)

    @pl.when(early)
    def _():
        sum_x.start()
        for i in range(shards // 2, shards):
            weigh_turned(i)

    trs[j] = tpart[j]
    time_rs.start(tpart)

    @pl.when(early)
    def _():
        lam_rs.start()

    pl.when(jnp.logical_not(early))(local_weights)
    @pl.when(early)
    def _():
        sum_x.wait()
        uz_buf[uz] = sum_x.total()
        hear()
        sum_z.start()

    @pl.when(jnp.logical_not(early))
    def _():
        hear()

    time_rs.wait()
    tzh[dh, 0] = time_rs.total(0, early_ranks)
    tzh[dh, 1] = time_rs.total(early_ranks, shards)
    time_zh.start()
    lam_rs.wait()
    lzh[dh] = lam_rs.total(0, early_ranks)
    lam_zh.start()

    @pl.when(early)
    def _():
        sum_z.wait()
        sums = sum_z.total()
        stat_buf[...] = sums[:, 2 * days:]
        unit_norm = sums[:, 2 * days:2 * days + 1]
        treat_count = jnp.maximum(sums[:, 2 * days + 1:2 * days + 2], 1.0)
        residual = (sums[:, 0:days] / unit_norm - sums[:, days:2 * days] / treat_count) * before
        res_left = jnp.concatenate(halves(residual), axis=0).astype(bf16)
        for i in range(early_ranks):
            cols = slice(i * own_units, (i + 1) * own_units)
            out = dot_nn(res_left, high_turned[:, cols]) + dot_nn(res_left, low_turned[:, cols])
            upart[i] = out[0:groups] + out[groups:]
        urs[j] = upart[j]
        unit_rs.start(upart)

    time_zh.wait()
    lam_zh.wait()
    lam_sum = to_col(lam_zh.total(), groups)
    both = time_zh.total()
    tag[j] = (both[0] / lam_sum - both[1]) * control_buf[j]
    time_ag.start()

    @pl.when(early)
    def _():
        unit_rs.wait()
        uzh[dh] = unit_rs.total()
        unit_zh.start()

        time_ag.wait()
        for i in range(shards):
            left_buf[0:2 * groups, i * shard:(i + 1) * shard] = jnp.concatenate(
                halves(tag[i]), axis=0
            ).astype(bf16)
        left = left_buf[0:2 * groups, :]
        acc = dot_nn(left, high_buf[...]) + dot_nn(left, low_buf[...])
        grad[u] = acc[0:groups] + acc[groups:]
        time_grad.start()

    @pl.when(early)
    def _():
        unit_zh.wait()
        updated = raised_buf[j] / stat_buf[:, 0:1] * jnp.exp(-step_rate * unit_zh.total() / jnp.sqrt(before_len))
        uag[j] = updated
        utot[u] = to_row(jnp.sum(updated, axis=1, keepdims=True))
        unit_tot.start()
        unit_ag.start()

        time_grad.wait()
        ctrl_root = jnp.sqrt(jnp.maximum(stat_buf[:, 2:3], 1.0))
        moved = moved_buf[...] / lam_sum * jnp.exp(-step_rate * time_grad.total() / ctrl_root)
        moved_buf[...] = moved
        ttot[d] = to_row(jnp.sum(moved, axis=1, keepdims=True))
        time_tot.start()

        unit_tot.wait()
        uall[j] = unit_tot.total() + to_row(stat_buf[:, 2:3], groups)
        unit_all.start()

    unit_ag.wait()
    unit_all.wait()
    unit_total = jnp.broadcast_to(to_col(unit_all.total(0, early_ranks), groups), (groups, own_units))
    count = jnp.broadcast_to(to_col(uall[0], groups, groups), (groups, own_units))
    for i in range(early_ranks):
        unit_out[:, i * own_units:(i + 1) * own_units] = uag[i] / unit_total * count

    @pl.when(early)
    def _():
        time_tot.wait()
        time_out[...] = moved_buf[...] / to_col(time_tot.total(), groups) * before_len

    @pl.when(jnp.logical_not(early))
    def _():
        time_out[...] = jnp.zeros_like(time_out)

    for group in (time_rs, time_zh, lam_zh, time_ag):
        group.drain()

    @pl.when(early)
    def _():
        for group in (lam_rs, sum_x, sum_z, unit_rs, unit_zh, unit_tot, unit_ag, unit_all, time_grad, time_tot):
            group.drain()


def put_out(unit_in, time_in, unit_out, time_out, sems):
    copies = [
        pltpu.make_async_copy(unit_in, unit_out, sems.at[0]),
        pltpu.make_async_copy(time_in, time_out, sems.at[1]),
    ]
    for copy in copies:
        copy.start()
    for copy in copies:
        copy.wait()


def local(unit_split, day_split, outcomes, cohort, pre_end, post_start, unit_logit, time_logit):
    groups = pre_end.shape[0]
    units, days = outcomes.shape
    nx, nz = unit_split
    ny, nh, nc = day_split
    unit_n, day_n, shards = nx * nz, ny * nh * nc, ny * nc
    shard = units // shards
    own = shards // 2
    hbm = pl.BlockSpec(memory_space=pl.ANY)
    vmem = pl.BlockSpec(memory_space=pltpu.VMEM)
    dma = lambda n: pltpu.SemaphoreType.DMA((n,))
    slots = lambda n, size: pltpu.VMEM((n, groups, size), f32)
    rows = lambda n: pltpu.VMEM((n, 1, LANES), f32)
    unit_weights, time_weights = pl.pallas_call(
        functools.partial(kernel, unit_split, day_split),
        out_shape=(pltpu.VMEM((groups, units), f32), pltpu.VMEM((groups, days), f32)),
        in_specs=[hbm] * 6,
        out_specs=(vmem, vmem),
        scratch_shapes=[
            pltpu.SMEM((groups,), jnp.int32),
            pltpu.SMEM((groups,), jnp.int32),
            pltpu.VMEM((1, units), jnp.int32),
            pltpu.VMEM((groups, units), f32),
            pltpu.VMEM((groups, days), f32),
            pltpu.VMEM((units, days), f32),
            pltpu.VMEM((units, days), bf16),
            pltpu.VMEM((units, days), bf16),
            pltpu.VMEM((days, units), bf16),
            pltpu.VMEM((days, units), bf16),
            pltpu.VMEM((4 * groups, units), bf16),
            slots(own, units // own), slots(shards, shard),
            pltpu.VMEM((groups, days), f32),
            pltpu.VMEM((groups, LANES), f32),
            slots(nx, 2 * days + LANES), slots(nz, 2 * days + LANES), slots(unit_n, days),
            slots(own, units // own), slots(own, units // own), slots(nh, units // own), slots(shards, units // own),
            slots(shards, shard), slots(shards, shard),
            pltpu.VMEM((nh, 2, groups, shard), f32),
            slots(shards, shard),
            rows(shards), rows(nh), rows(unit_n), rows(shards), rows(day_n // 2),
            dma(5),
            dma(PARTS),
            pltpu.SemaphoreType.REGULAR((2,)),
            *[dma(2)] * 14,
        ],
        compiler_params=pltpu.CompilerParams(collective_id=0, has_side_effects=True),
    )(pre_end, post_start, outcomes, cohort.reshape(1, units), unit_logit, time_logit)
    return pl.pallas_call(
        put_out,
        out_shape=(
            jax.ShapeDtypeStruct((groups, units), f32),
            jax.ShapeDtypeStruct((groups, days), f32),
        ),
        in_specs=[vmem] * 2,
        out_specs=(hbm, hbm),
        scratch_shapes=[dma(2)],
    )(*(pltpu.with_memory_space_constraint(v, pltpu.VMEM) for v in (unit_weights, time_weights)))


def solution(mesh):
    return jax.shard_map(
        functools.partial(local, UNIT_SPLIT, DAY_SPLIT),
        mesh=mesh,
        in_specs=(P("unit", "day"), P("unit"), P(), P(), P(None, "unit"), P(None, "day")),
        out_specs=(P(None, "unit"), P(None, "day")),
        check_vma=False,
    )
```

```python
import functools

import jax
import jax.numpy as jnp
from jax import lax
from jax.experimental import pallas as pl
from jax.experimental.pallas import tpu as pltpu
from jax.sharding import PartitionSpec as P

MESH = pl.DeviceIdType.MESH
step_rate = 16.0
CHUNK = 256
PARTS = 4
LANES = 128
UNIT_SPLIT = (4, 4)
DAY_SPLIT = (4, 2, 2)
f32, bf16 = jnp.float32, jnp.bfloat16


def dot_nn(a, b):
    return jnp.dot(a, b, preferred_element_type=f32)


def dot_nt(a, b):
    return lax.dot_general(a, b, (((1,), (1,)), ((), ())), preferred_element_type=f32)


def halves(v):
    high = v.astype(bf16).astype(f32)
    return high, v - high


def to_row(col, first=0):
    groups = col.shape[0]
    row_id = lax.broadcasted_iota(jnp.int32, (groups, LANES), 0)
    lane_id = lax.broadcasted_iota(jnp.int32, (groups, LANES), 1)
    return jnp.sum(jnp.where(row_id + first == lane_id, col, 0.0), axis=0, keepdims=True)


def to_col(row, groups, first=0):
    row_id = lax.broadcasted_iota(jnp.int32, (groups, LANES), 0)
    lane_id = lax.broadcasted_iota(jnp.int32, (groups, LANES), 1)
    return jnp.sum(jnp.where(row_id + first == lane_id, row, 0.0), axis=1, keepdims=True)


def column(ref, groups):
    row_id = lax.broadcasted_iota(jnp.int32, (groups, 1), 0)
    out = jnp.zeros((groups, 1), jnp.int32)
    for g in range(groups):
        out = jnp.where(row_id == g, ref[g], out)
    return out


class Exchange:
    def __init__(self, buf, sems, rank, size, place, takes=None, flag=None, sent=None, taken=None):
        self.buf, self.sems = buf, sems
        self.rank, self.size, self.place = rank, size, place
        self.takes, self.flag = takes, flag
        self.sent = size - 1 if sent is None else sent
        self.taken = size - 1 if taken is None else taken

    def copy(self, src, dst, peer):
        return pltpu.make_async_remote_copy(
            src_ref=src, dst_ref=dst, send_sem=self.sems.at[0], recv_sem=self.sems.at[1],
            device_id=self.place(peer), device_id_type=MESH,
        )

    def start(self, source=None):
        own = self.buf.at[self.rank]
        for k in range(1, self.size):
            peer = lax.rem(self.rank + k, self.size)

            def act(peer=peer):
                self.copy(own if source is None else source.at[peer], own, peer).start()

            if self.takes is None:
                act()
            else:
                pl.when(self.takes(peer))(act)

    def all_of(self, count, act):
        def some(n):
            if n:
                slots = self.buf.at[pl.ds(0, n)]
                act(self.copy(slots, slots, lax.rem(self.rank + 1, self.size)))

        if isinstance(count, tuple):
            pl.when(self.flag)(lambda: some(count[0]))
            pl.when(jnp.logical_not(self.flag))(lambda: some(count[1]))
        else:
            some(count)

    def drain(self):
        self.all_of(self.sent, lambda copy: copy.wait_send())

    def wait(self):
        self.all_of(self.taken, lambda copy: copy.wait_recv())

    def total(self, low=0, high=None):
        out = self.buf[low]
        for i in range(low + 1, self.size if high is None else high):
            out = out + self.buf[i]
        return out


class Total:
    def copy(self, own, place):
        return pltpu.make_async_remote_copy(
            src_ref=own, dst_ref=own, send_sem=self.sems.at[0], recv_sem=self.sems.at[1],
            device_id=place, device_id_type=MESH,
        )

    def some(self, n):
        slots = self.buf.at[pl.ds(0, n)]
        return self.copy(slots, self.any_peer)

    def wait(self):
        self.some(self.members - 1).wait_recv()

    def total(self):
        out = self.buf[0]
        for i in range(1, self.members):
            out = out + self.buf[i]
        return out


class RingTotal(Total):
    def __init__(self, buf, sems, ux, uz, dy, nx, nz, ny, steps, on_ring):
        self.buf, self.sems, self.members = buf, sems, nx * nz * ny
        self.ux, self.dy, self.own = ux, dy, (ux * nz + uz) * ny + dy
        self.nx, self.ny, self.steps, self.on_ring = nx, ny, steps, on_ring
        self.any_peer = on_ring(ux, 1)

    def start(self):
        own = self.buf.at[self.own]
        for step in (0,) + self.steps:
            for k in range(self.nx):
                for i in range(self.ny):
                    if step or k or i:
                        x, y = lax.rem(self.ux + k, self.nx), lax.rem(self.dy + i, self.ny)
                        self.copy(own, self.on_ring(x, -step, y)).start()

    def drain(self):
        self.some(self.members - 1).wait_send()


class CoreTotal(Total):
    def __init__(self, buf, sems, ux, uz, dy, dh, dc, ny, nc, flag, at):
        self.buf, self.sems, self.members, self.flag = buf, sems, nc, flag
        self.dc, self.nc = dc, nc
        self.beside = lambda c: at(ux, uz, dy, dh, c)
        self.across = lambda c: at(ux, uz, ny - 1 - dy, dh, c)
        self.any_peer = self.across(dc)

    def start(self):
        own = self.buf.at[self.dc]
        for k in range(1, self.nc):
            self.copy(own, self.beside(lax.rem(self.dc + k, self.nc))).start()
        for c in range(self.nc):
            self.copy(own, self.across(c)).start()

    def wait(self):
        if self.nc > 1:
            pl.when(self.flag)(lambda: self.some(self.nc - 1).wait_recv())
        pl.when(jnp.logical_not(self.flag))(lambda: self.some(self.nc).wait_recv())

    def drain(self):
        self.some(2 * self.nc - 1).wait_send()


class DayTotal(Total):
    def __init__(self, buf, sems, ux, uz, dy, dh, dc, nz, ny, nh, nc, at):
        self.buf, self.sems, self.members = buf, sems, ny * nh * nc
        self.ux, self.uz, self.dy, self.dh, self.dc, self.nz, self.ny, self.nh, self.nc, self.at = (
            ux, uz, dy, dh, dc, nz, ny, nh, nc, at
        )
        self.own = dy * (nh * nc) + dh * nc + dc
        self.rank, self.ranks = dy * nc + dc, ny * nc
        self.any_peer = at(ux, uz, dy, 1 - dh, dc)

    def start(self):
        own = self.buf.at[self.own]
        for k in range(1, self.ranks):
            peer = lax.rem(self.rank + k, self.ranks)
            self.copy(own, self.at(self.ux, self.uz, lax.div(peer, self.nc), self.dh, lax.rem(peer, self.nc))).start()
        for end, firsts in ((self.nz - 1, range(self.nz // 2)), (0, range(self.nz // 2, self.nz))):

            @pl.when(self.uz == end)
            def _(firsts=firsts):
                for q in firsts:
                    for k in range(self.ranks):
                        self.copy(own, self.at(self.ux, q, k // self.nc, 1 - self.dh, k % self.nc)).start()

    def drain(self):
        self.some(self.ranks - 1).wait_send()

        @pl.when((self.uz == 0) | (self.uz == self.nz - 1))
        def _():
            self.some(self.nz // 2 * self.ranks).wait_send()


def kernel(
    unit_split, day_split,
    pre_hbm, post_hbm, x_hbm, cohort_hbm, unit_logit_hbm, time_logit_hbm,
    unit_out, time_out,
    pre_ref, post_ref, cohort_ref, unit_logit_ref, time_logit_ref,
    x_buf, high_buf, low_buf, high_turned, low_turned, left_buf, raised_buf, control_buf, moved_buf,
    stat_buf, ux_buf, uz_buf, grad,
    upart, urs, uzh, uag, tpart, trs, tzh, tag, lrs, lzh, utot, uall, ttot,
    in_sem, x_sem, near_sem, ux_sem, uz_sem, grad_sem,
    urs_sem, uzh_sem, uag_sem, trs_sem, tzh_sem, tag_sem, lrs_sem, lzh_sem, utot_sem, uall_sem, ttot_sem,
):
    nx, nz = unit_split
    ny, nh, nc = day_split
    unit_n, day_n, shards = nx * nz, ny * nh * nc, ny * nc
    units, days = x_buf.shape
    groups = unit_logit_ref.shape[0]
    shard = units // shards
    own_units = units // (shards // 2)
    all_count = day_n * days
    early_ranks = shards // 2

    u, d = lax.axis_index("unit"), lax.axis_index("day")
    ux, uz = lax.div(u, nz), lax.rem(u, nz)
    dy, dh, dc = lax.div(d, nh * nc), lax.rem(lax.div(d, nc), nh), lax.rem(d, nc)
    j = dy * nc + dc
    early = j < early_ranks

    def in_shards(rank):
        return {"day": lax.div(rank, nc) * (nh * nc) + dh * nc + lax.rem(rank, nc)}

    def in_high(rank):
        return {"day": dy * (nh * nc) + rank * nc + dc}

    def at(x, z, y, h, c):
        return {"unit": x * nz + z, "day": y * (nh * nc) + h * nc + c}

    ring = nh * nz
    ring_steps = tuple(k for k in range(-(nz // 2) + 1, nz // 2 + 1) if k)

    def on_ring(x, step, y=None):
        z = lax.rem(dh * nz + uz + step + ring, ring)
        return at(x, lax.rem(z, nz), dy if y is None else y, lax.div(z, nz), dc)

    on_unit = lambda rank: {"unit": rank}
    on_x = lambda rank: {"unit": rank * nz + uz}
    on_z = lambda rank: {"unit": ux * nz + rank}

    barrier = pltpu.get_barrier_semaphore()

    def greet(place):
        pl.semaphore_signal(barrier, inc=1, device_id=place, device_id_type=MESH)

    for k in range(1, shards):
        greet(in_shards(lax.rem(j + k, shards)))
    for step in (-2, -1, 1, 2):
        greet(on_ring(ux, step))

    @pl.when(early)
    def _():
        for k in range(1, nx):
            greet(on_x(lax.rem(ux + k, nx)))

    inputs = [
        pltpu.make_async_copy(src, dst, in_sem.at[k])
        for k, (src, dst) in enumerate((
            (time_logit_hbm, time_logit_ref), (pre_hbm, pre_ref), (post_hbm, post_ref),
            (unit_logit_hbm, unit_logit_ref), (cohort_hbm, cohort_ref),
        ))
    ]
    part = units // PARTS
    loads = [
        pltpu.make_async_copy(x_hbm.at[pl.ds(k * part, part)], x_buf.at[pl.ds(k * part, part)], x_sem.at[k])
        for k in range(PARTS)
    ]
    for copy in inputs + loads:
        copy.start()

    sum_x = Exchange(ux_buf, ux_sem, ux, nx, on_x)
    sum_z = Exchange(uz_buf, uz_sem, uz, nz, on_z)
    to_early = (early_ranks - 1, early_ranks)
    from_early = dict(flag=early, taken=to_early)
    unit_rs = Exchange(urs, urs_sem, j, early_ranks, in_shards)
    unit_zh = Exchange(uzh, uzh_sem, dh, nh, in_high)
    unit_ag = Exchange(uag, uag_sem, j, shards, in_shards, **from_early)
    unit_tot = RingTotal(utot, utot_sem, ux, uz, dy, nx, nz, ny // 2, ring_steps, on_ring)
    unit_all = CoreTotal(uall, uall_sem, ux, uz, dy, dh, dc, ny, nc, early, at)
    time_rs = Exchange(trs, trs_sem, j, shards, in_shards)
    time_zh = Exchange(tzh, tzh_sem, dh, nh, in_high)
    time_ag = Exchange(
        tag, tag_sem, j, shards, in_shards, takes=lambda rank: rank < early_ranks, flag=early, sent=to_early
    )
    lam_rs = Exchange(lrs, lrs_sem, j, shards, in_shards, **from_early)
    lam_zh = Exchange(lzh, lzh_sem, dh, nh, in_high)
    time_grad = Exchange(grad, grad_sem, u, unit_n, on_unit)
    time_tot = DayTotal(ttot, ttot_sem, ux, uz, dy, dh, dc, nz, ny // 2, nh, nc, at)

    for copy in inputs[:3]:
        copy.wait()
    pre_end, post_start = column(pre_ref, groups), column(post_ref, groups)
    before_len = pre_end.astype(f32)
    after_len = (all_count - post_start).astype(f32)
    day_index = d * days + lax.broadcasted_iota(jnp.int32, (groups, days), 1)
    before = jnp.where(day_index < pre_end, 1.0, 0.0)
    after = jnp.where(day_index >= post_start, 1.0, 0.0)
    time_raised = jnp.exp(time_logit_ref[...]) * before
    moved_buf[...] = time_raised
    time_left = jnp.concatenate(halves(time_raised + after), axis=0).astype(bf16)
    scale = jnp.broadcast_to(jnp.where(early, 1.0, 1.0 / after_len), (groups, shard))
    lrs[j] = to_row(jnp.sum(time_raised, axis=1, keepdims=True))

    def hear():
        pl.semaphore_wait(near_sem.at[0], 1)
        pl.semaphore_wait(near_sem.at[1], 1)

    def split(k):
        rows = pl.ds(k * part, part)
        whole = x_buf[rows, :]
        high = whole.astype(bf16)
        high_buf[rows, :] = high
        low_buf[rows, :] = (whole - high.astype(f32)).astype(bf16)

    def weigh_units(k):
        for i in range(k * part // shard, (k + 1) * part // shard):
            rows = pl.ds(i * shard, shard)
            out = dot_nt(time_left, high_buf[rows, :]) + dot_nt(time_left, low_buf[rows, :])
            tpart[i] = (out[0:groups] + out[groups:]) * scale

    def local_weights():
        for copy in inputs[3:]:
            copy.wait()

        labels = lax.broadcasted_iota(jnp.int32, (groups, units), 0)
        cohort = jnp.broadcast_to(cohort_ref[...], (groups, units))
        treated = jnp.where(cohort == labels, 1.0, 0.0)
        control = jnp.where(cohort > labels, 1.0, 0.0)
        raised = jnp.exp(unit_logit_ref[...]) * control
        for i in range(shards):
            control_buf[i] = control[:, i * shard:(i + 1) * shard]
        for i in range(early_ranks):
            raised_buf[i] = raised[:, i * own_units:(i + 1) * own_units]
        raised_high, raised_low = halves(raised)
        left_buf[...] = jnp.concatenate(
            [raised_high, raised_low, treated, jnp.zeros_like(treated)], axis=0
        ).astype(bf16)
        norm_part = jnp.sum(raised, axis=1, keepdims=True)
        treat_part = jnp.sum(treated, axis=1, keepdims=True)
        ctrl_part = jnp.sum(control, axis=1, keepdims=True)
        lane = lax.broadcasted_iota(jnp.int32, (groups, LANES), 1)
        ux_buf[ux, :, 2 * days:] = jnp.where(
            lane == 0, norm_part, jnp.where(lane == 1, treat_part, jnp.where(lane == 2, ctrl_part, 0.0))
        )

    for k in range(PARTS):
        loads[k].wait()
        if k:
            weigh_units(k - 1)
        split(k)
        if k == 2:
            pl.when(early)(local_weights)
    weigh_units(PARTS - 1)
    trs[j] = tpart[j]

    pl.semaphore_wait(barrier, shards - 1 + 4 + jnp.where(early, nx - 1, 0))
    pl.semaphore_signal(near_sem.at[0], inc=1, device_id=on_ring(ux, 2), device_id_type=MESH)
    pl.semaphore_signal(near_sem.at[1], inc=1, device_id=on_ring(ux, -2), device_id_type=MESH)

    time_rs.start(tpart)

    @pl.when(early)
    def _():
        lam_rs.start()
        acc = dot_nn(left_buf[...], high_buf[...]) + dot_nn(left_buf[...], low_buf[...])
        ux_buf[ux, :, 0:days] = acc[0:groups] + acc[groups:2 * groups]
        ux_buf[ux, :, days:2 * days] = acc[2 * groups:3 * groups]
        sum_x.start()
        for k in range(units // CHUNK):
            rows = pl.ds(k * CHUNK, CHUNK)
            high_turned[:, k * CHUNK:(k + 1) * CHUNK] = high_buf[rows, :].T
            low_turned[:, k * CHUNK:(k + 1) * CHUNK] = low_buf[rows, :].T

    pl.when(jnp.logical_not(early))(local_weights)
    @pl.when(early)
    def _():
        sum_x.wait()
        uz_buf[uz] = sum_x.total()
        hear()
        sum_z.start()

    @pl.when(jnp.logical_not(early))
    def _():
        hear()

    time_rs.wait()
    tzh[dh, 0] = time_rs.total(0, early_ranks)
    tzh[dh, 1] = time_rs.total(early_ranks, shards)
    time_zh.start()
    lam_rs.wait()
    lzh[dh] = lam_rs.total(0, early_ranks)
    lam_zh.start()

    @pl.when(early)
    def _():
        sum_z.wait()
        sums = sum_z.total()
        stat_buf[...] = sums[:, 2 * days:]
        unit_norm = sums[:, 2 * days:2 * days + 1]
        treat_count = jnp.maximum(sums[:, 2 * days + 1:2 * days + 2], 1.0)
        residual = (sums[:, 0:days] / unit_norm - sums[:, days:2 * days] / treat_count) * before
        res_left = jnp.concatenate(halves(residual), axis=0).astype(bf16)
        for i in range(early_ranks):
            cols = slice(i * own_units, (i + 1) * own_units)
            out = dot_nn(res_left, high_turned[:, cols]) + dot_nn(res_left, low_turned[:, cols])
            upart[i] = out[0:groups] + out[groups:]
        urs[j] = upart[j]
        unit_rs.start(upart)

    time_zh.wait()
    lam_zh.wait()
    lam_sum = to_col(lam_zh.total(), groups)
    both = time_zh.total()
    tag[j] = (both[0] / lam_sum - both[1]) * control_buf[j]
    time_ag.start()

    @pl.when(early)
    def _():
        unit_rs.wait()
        uzh[dh] = unit_rs.total()
        unit_zh.start()

        time_ag.wait()
        for i in range(shards):
            left_buf[0:2 * groups, i * shard:(i + 1) * shard] = jnp.concatenate(
                halves(tag[i]), axis=0
            ).astype(bf16)
        left = left_buf[0:2 * groups, :]
        acc = dot_nn(left, high_buf[...]) + dot_nn(left, low_buf[...])
        grad[u] = acc[0:groups] + acc[groups:]
        time_grad.start()

    @pl.when(early)
    def _():
        unit_zh.wait()
        updated = raised_buf[j] / stat_buf[:, 0:1] * jnp.exp(-step_rate * unit_zh.total() / jnp.sqrt(before_len))
        uag[j] = updated
        utot[unit_tot.own] = to_row(jnp.sum(updated, axis=1, keepdims=True))
        unit_tot.start()
        unit_ag.start()

        time_grad.wait()
        ctrl_root = jnp.sqrt(jnp.maximum(stat_buf[:, 2:3], 1.0))
        moved = moved_buf[...] / lam_sum * jnp.exp(-step_rate * time_grad.total() / ctrl_root)
        moved_buf[...] = moved
        ttot[d] = to_row(jnp.sum(moved, axis=1, keepdims=True))
        time_tot.start()

        unit_tot.wait()
        uall[dc] = unit_tot.total() + to_row(stat_buf[:, 2:3], groups)
        unit_all.start()

    unit_ag.wait()
    unit_all.wait()
    unit_total = jnp.broadcast_to(to_col(unit_all.total(), groups), (groups, own_units))
    count = jnp.broadcast_to(to_col(uall[0], groups, groups), (groups, own_units))
    for i in range(early_ranks):
        unit_out[:, i * own_units:(i + 1) * own_units] = uag[i] / unit_total * count

    @pl.when(early)
    def _():
        time_tot.wait()
        time_out[...] = moved_buf[...] / to_col(time_tot.total(), groups) * before_len

    @pl.when(jnp.logical_not(early))
    def _():
        time_out[...] = jnp.zeros_like(time_out)

    for group in (time_rs, time_zh, lam_zh, time_ag):
        group.drain()

    @pl.when(early)
    def _():
        for group in (lam_rs, sum_x, sum_z, unit_rs, unit_zh, unit_tot, unit_ag, unit_all, time_grad, time_tot):
            group.drain()


def put_out(unit_in, time_in, unit_out, time_out, sems):
    copies = [
        pltpu.make_async_copy(unit_in, unit_out, sems.at[0]),
        pltpu.make_async_copy(time_in, time_out, sems.at[1]),
    ]
    for copy in copies:
        copy.start()
    for copy in copies:
        copy.wait()


def local(unit_split, day_split, outcomes, cohort, pre_end, post_start, unit_logit, time_logit):
    groups = pre_end.shape[0]
    units, days = outcomes.shape
    nx, nz = unit_split
    ny, nh, nc = day_split
    unit_n, day_n, shards = nx * nz, ny * nh * nc, ny * nc
    shard = units // shards
    own = shards // 2
    hbm = pl.BlockSpec(memory_space=pl.ANY)
    vmem = pl.BlockSpec(memory_space=pltpu.VMEM)
    dma = lambda n: pltpu.SemaphoreType.DMA((n,))
    slots = lambda n, size: pltpu.VMEM((n, groups, size), f32)
    rows = lambda n: pltpu.VMEM((n, 1, LANES), f32)
    unit_weights, time_weights = pl.pallas_call(
        functools.partial(kernel, unit_split, day_split),
        out_shape=(pltpu.VMEM((groups, units), f32), pltpu.VMEM((groups, days), f32)),
        in_specs=[hbm] * 6,
        out_specs=(vmem, vmem),
        scratch_shapes=[
            pltpu.SMEM((groups,), jnp.int32),
            pltpu.SMEM((groups,), jnp.int32),
            pltpu.VMEM((1, units), jnp.int32),
            pltpu.VMEM((groups, units), f32),
            pltpu.VMEM((groups, days), f32),
            pltpu.VMEM((units, days), f32),
            pltpu.VMEM((units, days), bf16),
            pltpu.VMEM((units, days), bf16),
            pltpu.VMEM((days, units), bf16),
            pltpu.VMEM((days, units), bf16),
            pltpu.VMEM((4 * groups, units), bf16),
            slots(own, units // own), slots(shards, shard),
            pltpu.VMEM((groups, days), f32),
            pltpu.VMEM((groups, LANES), f32),
            slots(nx, 2 * days + LANES), slots(nz, 2 * days + LANES), slots(unit_n, days),
            slots(own, units // own), slots(own, units // own), slots(nh, units // own), slots(shards, units // own),
            slots(shards, shard), slots(shards, shard),
            pltpu.VMEM((nh, 2, groups, shard), f32),
            slots(shards, shard),
            rows(shards), rows(nh), rows(unit_n * ny // 2), rows(2 * nc), rows(day_n // 2),
            dma(5),
            dma(PARTS),
            pltpu.SemaphoreType.REGULAR((2,)),
            *[dma(2)] * 14,
        ],
        compiler_params=pltpu.CompilerParams(collective_id=0, has_side_effects=True),
    )(pre_end, post_start, outcomes, cohort.reshape(1, units), unit_logit, time_logit)
    return pl.pallas_call(
        put_out,
        out_shape=(
            jax.ShapeDtypeStruct((groups, units), f32),
            jax.ShapeDtypeStruct((groups, days), f32),
        ),
        in_specs=[vmem] * 2,
        out_specs=(hbm, hbm),
        scratch_shapes=[dma(2)],
    )(*(pltpu.with_memory_space_constraint(v, pltpu.VMEM) for v in (unit_weights, time_weights)))


def solution(mesh):
    return jax.shard_map(
        functools.partial(local, UNIT_SPLIT, DAY_SPLIT),
        mesh=mesh,
        in_specs=(P("unit", "day"), P("unit"), P(), P(), P(None, "unit"), P(None, "day")),
        out_specs=(P(None, "unit"), P(None, "day")),
        check_vma=False,
    )
```

```python
import functools

import jax
import jax.numpy as jnp
from jax import lax
from jax.experimental import pallas as pl
from jax.experimental.pallas import tpu as pltpu
from jax.sharding import PartitionSpec as P

MESH = pl.DeviceIdType.MESH
step_rate = 16.0
CHUNK = 256
PARTS = 4
LANES = 128
UNIT_SPLIT = (4, 4)
DAY_SPLIT = (4, 2, 2)
f32, bf16 = jnp.float32, jnp.bfloat16


def dot_nn(a, b):
    return jnp.dot(a, b, preferred_element_type=f32)


def dot_nt(a, b):
    return lax.dot_general(a, b, (((1,), (1,)), ((), ())), preferred_element_type=f32)


def halves(v):
    high = v.astype(bf16).astype(f32)
    return high, v - high


def to_row(col, first=0):
    groups = col.shape[0]
    row_id = lax.broadcasted_iota(jnp.int32, (groups, LANES), 0)
    lane_id = lax.broadcasted_iota(jnp.int32, (groups, LANES), 1)
    return jnp.sum(jnp.where(row_id + first == lane_id, col, 0.0), axis=0, keepdims=True)


def to_col(row, groups, first=0):
    row_id = lax.broadcasted_iota(jnp.int32, (groups, LANES), 0)
    lane_id = lax.broadcasted_iota(jnp.int32, (groups, LANES), 1)
    return jnp.sum(jnp.where(row_id + first == lane_id, row, 0.0), axis=1, keepdims=True)


def column(ref, groups):
    row_id = lax.broadcasted_iota(jnp.int32, (groups, 1), 0)
    out = jnp.zeros((groups, 1), jnp.int32)
    for g in range(groups):
        out = jnp.where(row_id == g, ref[g], out)
    return out


class Exchange:
    def __init__(self, buf, sems, rank, size, place, takes=None, flag=None, sent=None, taken=None):
        self.buf, self.sems = buf, sems
        self.rank, self.size, self.place = rank, size, place
        self.takes, self.flag = takes, flag
        self.sent = size - 1 if sent is None else sent
        self.taken = size - 1 if taken is None else taken

    def copy(self, src, dst, peer):
        return pltpu.make_async_remote_copy(
            src_ref=src, dst_ref=dst, send_sem=self.sems.at[0], recv_sem=self.sems.at[1],
            device_id=self.place(peer), device_id_type=MESH,
        )

    def start(self, source=None):
        own = self.buf.at[self.rank]
        for k in range(1, self.size):
            peer = lax.rem(self.rank + k, self.size)

            def act(peer=peer):
                self.copy(own if source is None else source.at[peer], own, peer).start()

            if self.takes is None:
                act()
            else:
                pl.when(self.takes(peer))(act)

    def all_of(self, count, act):
        def some(n):
            if n:
                slots = self.buf.at[pl.ds(0, n)]
                act(self.copy(slots, slots, lax.rem(self.rank + 1, self.size)))

        if isinstance(count, tuple):
            pl.when(self.flag)(lambda: some(count[0]))
            pl.when(jnp.logical_not(self.flag))(lambda: some(count[1]))
        else:
            some(count)

    def drain(self):
        self.all_of(self.sent, lambda copy: copy.wait_send())

    def wait(self):
        self.all_of(self.taken, lambda copy: copy.wait_recv())

    def total(self, low=0, high=None):
        out = self.buf[low]
        for i in range(low + 1, self.size if high is None else high):
            out = out + self.buf[i]
        return out


class Total:
    def copy(self, own, place):
        return pltpu.make_async_remote_copy(
            src_ref=own, dst_ref=own, send_sem=self.sems.at[0], recv_sem=self.sems.at[1],
            device_id=place, device_id_type=MESH,
        )

    def some(self, n):
        slots = self.buf.at[pl.ds(0, n)]
        return self.copy(slots, self.any_peer)

    def wait(self):
        self.some(self.members - 1).wait_recv()

    def total(self):
        out = self.buf[0]
        for i in range(1, self.members):
            out = out + self.buf[i]
        return out


class RingTotal(Total):
    def __init__(self, buf, sems, ux, uz, dy, nx, nz, ny, steps, on_ring):
        self.buf, self.sems, self.members = buf, sems, nx * nz * ny
        self.ux, self.dy, self.own = ux, dy, (ux * nz + uz) * ny + dy
        self.nx, self.ny, self.steps, self.on_ring = nx, ny, steps, on_ring
        self.any_peer = on_ring(ux, 1)

    def start(self):
        own = self.buf.at[self.own]
        for step in (0,) + self.steps:
            for k in range(self.nx):
                for i in range(self.ny):
                    if step or k or i:
                        x, y = lax.rem(self.ux + k, self.nx), lax.rem(self.dy + i, self.ny)
                        self.copy(own, self.on_ring(x, -step, y)).start()

    def drain(self):
        self.some(self.members - 1).wait_send()


class CoreTotal(Total):
    def __init__(self, buf, sems, ux, uz, dy, dh, dc, ny, nc, flag, at):
        self.buf, self.sems, self.members, self.flag = buf, sems, nc, flag
        self.dc, self.nc = dc, nc
        self.beside = lambda c: at(ux, uz, dy, dh, c)
        self.across = lambda c: at(ux, uz, ny - 1 - dy, dh, c)
        self.any_peer = self.across(dc)

    def start(self):
        own = self.buf.at[self.dc]
        for k in range(1, self.nc):
            self.copy(own, self.beside(lax.rem(self.dc + k, self.nc))).start()
        for c in range(self.nc):
            self.copy(own, self.across(c)).start()

    def wait(self):
        if self.nc > 1:
            pl.when(self.flag)(lambda: self.some(self.nc - 1).wait_recv())
        pl.when(jnp.logical_not(self.flag))(lambda: self.some(self.nc).wait_recv())

    def drain(self):
        self.some(2 * self.nc - 1).wait_send()


class DayTotal(Total):
    def __init__(self, buf, sems, ux, uz, dy, dh, dc, nz, ny, nh, nc, at):
        self.buf, self.sems, self.members = buf, sems, ny * nh * nc
        self.ux, self.uz, self.dy, self.dh, self.dc, self.nz, self.ny, self.nh, self.nc, self.at = (
            ux, uz, dy, dh, dc, nz, ny, nh, nc, at
        )
        self.own = dy * (nh * nc) + dh * nc + dc
        self.rank, self.ranks = dy * nc + dc, ny * nc
        self.any_peer = at(ux, uz, dy, 1 - dh, dc)

    def start(self):
        own = self.buf.at[self.own]
        for k in range(1, self.ranks):
            peer = lax.rem(self.rank + k, self.ranks)
            self.copy(own, self.at(self.ux, self.uz, lax.div(peer, self.nc), self.dh, lax.rem(peer, self.nc))).start()
        for end, firsts in ((self.nz - 1, range(self.nz // 2)), (0, range(self.nz // 2, self.nz))):

            @pl.when(self.uz == end)
            def _(firsts=firsts):
                for q in firsts:
                    for k in range(self.ranks):
                        self.copy(own, self.at(self.ux, q, k // self.nc, 1 - self.dh, k % self.nc)).start()

    def drain(self):
        self.some(self.ranks - 1).wait_send()

        @pl.when((self.uz == 0) | (self.uz == self.nz - 1))
        def _():
            self.some(self.nz // 2 * self.ranks).wait_send()


def kernel(
    unit_split, day_split,
    pre_hbm, post_hbm, x_hbm, cohort_hbm, unit_logit_hbm, time_logit_hbm,
    unit_out, time_out,
    pre_ref, post_ref, cohort_ref, unit_logit_ref, time_logit_ref,
    x_buf, high_buf, low_buf, high_turned, low_turned, left_buf, raised_buf, control_buf, moved_buf,
    stat_buf, ux_buf, uz_buf, grad,
    upart, urs, uzh, uag, tpart, trs, tzh, tag, lrs, lzh, utot, uall, ttot,
    in_sem, x_sem, near_sem, ux_sem, uz_sem, grad_sem,
    urs_sem, uzh_sem, uag_sem, trs_sem, tzh_sem, tag_sem, lrs_sem, lzh_sem, utot_sem, uall_sem, ttot_sem,
):
    nx, nz = unit_split
    ny, nh, nc = day_split
    unit_n, day_n, shards = nx * nz, ny * nh * nc, ny * nc
    units, days = x_buf.shape
    groups = unit_logit_ref.shape[0]
    shard = units // shards
    own_units = units // (shards // 2)
    all_count = day_n * days
    early_ranks = shards // 2

    u, d = lax.axis_index("unit"), lax.axis_index("day")
    ux, uz = lax.div(u, nz), lax.rem(u, nz)
    dy, dh, dc = lax.div(d, nh * nc), lax.rem(lax.div(d, nc), nh), lax.rem(d, nc)
    j = dy * nc + dc
    early = j < early_ranks

    def in_shards(rank):
        return {"day": lax.div(rank, nc) * (nh * nc) + dh * nc + lax.rem(rank, nc)}

    def in_high(rank):
        return {"day": dy * (nh * nc) + rank * nc + dc}

    def at(x, z, y, h, c):
        return {"unit": x * nz + z, "day": y * (nh * nc) + h * nc + c}

    ring = nh * nz
    ring_steps = tuple(k for k in range(-(nz // 2) + 1, nz // 2 + 1) if k)

    def on_ring(x, step, y=None):
        z = lax.rem(dh * nz + uz + step + ring, ring)
        return at(x, lax.rem(z, nz), dy if y is None else y, lax.div(z, nz), dc)

    on_unit = lambda rank: {"unit": rank}
    on_x = lambda rank: {"unit": rank * nz + uz}
    on_z = lambda rank: {"unit": ux * nz + rank}

    barrier = pltpu.get_barrier_semaphore()

    def greet(place):
        pl.semaphore_signal(barrier, inc=1, device_id=place, device_id_type=MESH)

    for k in range(1, shards):
        greet(in_shards(lax.rem(j + k, shards)))
    for step in (-2, -1, 1, 2):
        greet(on_ring(ux, step))

    @pl.when(early)
    def _():
        for k in range(1, nx):
            greet(on_x(lax.rem(ux + k, nx)))

    inputs = [
        pltpu.make_async_copy(src, dst, in_sem.at[k])
        for k, (src, dst) in enumerate((
            (time_logit_hbm, time_logit_ref), (pre_hbm, pre_ref), (post_hbm, post_ref),
            (unit_logit_hbm, unit_logit_ref), (cohort_hbm, cohort_ref),
        ))
    ]
    part = units // PARTS
    loads = [
        pltpu.make_async_copy(x_hbm.at[pl.ds(k * part, part)], x_buf.at[pl.ds(k * part, part)], x_sem.at[k])
        for k in range(PARTS)
    ]
    for copy in inputs + loads:
        copy.start()

    sum_x = Exchange(ux_buf, ux_sem, ux, nx, on_x)
    sum_z = Exchange(uz_buf, uz_sem, uz, nz, on_z)
    to_early = (early_ranks - 1, early_ranks)
    from_early = dict(flag=early, taken=to_early)
    unit_rs = Exchange(urs, urs_sem, j, early_ranks, in_shards)
    unit_zh = Exchange(uzh, uzh_sem, dh, nh, in_high)
    unit_ag = Exchange(uag, uag_sem, j, shards, in_shards, **from_early)
    unit_tot = RingTotal(utot, utot_sem, ux, uz, dy, nx, nz, ny // 2, ring_steps, on_ring)
    unit_all = CoreTotal(uall, uall_sem, ux, uz, dy, dh, dc, ny, nc, early, at)
    time_rs = Exchange(trs, trs_sem, j, shards, in_shards)
    time_zh = Exchange(tzh, tzh_sem, dh, nh, in_high)
    time_ag = Exchange(
        tag, tag_sem, j, shards, in_shards, takes=lambda rank: rank < early_ranks, flag=early, sent=to_early
    )
    lam_rs = Exchange(lrs, lrs_sem, j, shards, in_shards, **from_early)
    lam_zh = Exchange(lzh, lzh_sem, dh, nh, in_high)
    time_grad = Exchange(grad, grad_sem, u, unit_n, on_unit)
    time_tot = DayTotal(ttot, ttot_sem, ux, uz, dy, dh, dc, nz, ny // 2, nh, nc, at)

    for copy in inputs[:3]:
        copy.wait()
    pre_end, post_start = column(pre_ref, groups), column(post_ref, groups)
    before_len = pre_end.astype(f32)
    after_len = (all_count - post_start).astype(f32)
    day_index = d * days + lax.broadcasted_iota(jnp.int32, (groups, days), 1)
    before = jnp.where(day_index < pre_end, 1.0, 0.0)
    after = jnp.where(day_index >= post_start, 1.0, 0.0)
    time_raised = jnp.exp(time_logit_ref[...]) * before
    moved_buf[...] = time_raised
    time_left = jnp.concatenate(halves(time_raised + after), axis=0).astype(bf16)
    scale = jnp.broadcast_to(jnp.where(early, 1.0, 1.0 / after_len), (groups, shard))
    lrs[j] = to_row(jnp.sum(time_raised, axis=1, keepdims=True))

    def hear():
        pl.semaphore_wait(near_sem.at[0], 1)
        pl.semaphore_wait(near_sem.at[1], 1)

    def split(k):
        rows = pl.ds(k * part, part)
        whole = x_buf[rows, :]
        high = whole.astype(bf16)
        high_buf[rows, :] = high
        low_buf[rows, :] = (whole - high.astype(f32)).astype(bf16)

    def weigh_units(k):
        for i in range(k * part // shard, (k + 1) * part // shard):
            rows = pl.ds(i * shard, shard)
            out = dot_nt(time_left, high_buf[rows, :]) + dot_nt(time_left, low_buf[rows, :])
            tpart[i] = (out[0:groups] + out[groups:]) * scale

    def local_weights():
        for copy in inputs[3:]:
            copy.wait()

        labels = lax.broadcasted_iota(jnp.int32, (groups, units), 0)
        cohort = jnp.broadcast_to(cohort_ref[...], (groups, units))
        treated = jnp.where(cohort == labels, 1.0, 0.0)
        control = jnp.where(cohort > labels, 1.0, 0.0)
        raised = jnp.exp(unit_logit_ref[...]) * control
        for i in range(shards):
            control_buf[i] = control[:, i * shard:(i + 1) * shard]
        for i in range(early_ranks):
            raised_buf[i] = raised[:, i * own_units:(i + 1) * own_units]
        raised_high, raised_low = halves(raised)
        left_buf[...] = jnp.concatenate(
            [raised_high, raised_low, treated, jnp.zeros_like(treated)], axis=0
        ).astype(bf16)
        norm_part = jnp.sum(raised, axis=1, keepdims=True)
        treat_part = jnp.sum(treated, axis=1, keepdims=True)
        ctrl_part = jnp.sum(control, axis=1, keepdims=True)
        lane = lax.broadcasted_iota(jnp.int32, (groups, LANES), 1)
        ux_buf[ux, :, 2 * days:] = jnp.where(
            lane == 0, norm_part, jnp.where(lane == 1, treat_part, jnp.where(lane == 2, ctrl_part, 0.0))
        )

    for k in range(PARTS):
        loads[k].wait()
        if k:
            weigh_units(k - 1)
        split(k)
        if k == 2:
            pl.when(early)(local_weights)
    weigh_units(PARTS - 1)
    trs[j] = tpart[j]

    pl.semaphore_wait(barrier, shards - 1 + 4 + jnp.where(early, nx - 1, 0))
    pl.semaphore_signal(near_sem.at[0], inc=1, device_id=on_ring(ux, 2), device_id_type=MESH)
    pl.semaphore_signal(near_sem.at[1], inc=1, device_id=on_ring(ux, -2), device_id_type=MESH)

    time_rs.start(tpart)

    @pl.when(early)
    def _():
        lam_rs.start()
        acc = dot_nn(left_buf[...], high_buf[...]) + dot_nn(left_buf[...], low_buf[...])
        ux_buf[ux, :, 0:days] = acc[0:groups] + acc[groups:2 * groups]
        ux_buf[ux, :, days:2 * days] = acc[2 * groups:3 * groups]
        sum_x.start()
        for k in range(units // CHUNK):
            rows = pl.ds(k * CHUNK, CHUNK)
            high_turned[:, k * CHUNK:(k + 1) * CHUNK] = high_buf[rows, :].T
            low_turned[:, k * CHUNK:(k + 1) * CHUNK] = low_buf[rows, :].T

    pl.when(jnp.logical_not(early))(local_weights)
    @pl.when(early)
    def _():
        sum_x.wait()
        uz_buf[uz] = sum_x.total()
        hear()
        sum_z.start()

    @pl.when(jnp.logical_not(early))
    def _():
        hear()

    time_rs.wait()
    tzh[dh, 0] = time_rs.total(0, early_ranks)
    tzh[dh, 1] = time_rs.total(early_ranks, shards)
    time_zh.start()
    lam_rs.wait()
    lzh[dh] = lam_rs.total(0, early_ranks)
    lam_zh.start()

    @pl.when(early)
    def _():
        sum_z.wait()
        sums = sum_z.total()
        stat_buf[...] = sums[:, 2 * days:]
        unit_norm = sums[:, 2 * days:2 * days + 1]
        treat_count = jnp.maximum(sums[:, 2 * days + 1:2 * days + 2], 1.0)
        residual = (sums[:, 0:days] / unit_norm - sums[:, days:2 * days] / treat_count) * before
        res_left = jnp.concatenate(halves(residual), axis=0).astype(bf16)
        for i in range(early_ranks):
            cols = slice(i * own_units, (i + 1) * own_units)
            out = dot_nn(res_left, high_turned[:, cols]) + dot_nn(res_left, low_turned[:, cols])
            upart[i] = out[0:groups] + out[groups:]
        urs[j] = upart[j]
        unit_rs.start(upart)

    time_zh.wait()
    lam_zh.wait()
    lam_sum = to_col(lam_zh.total(), groups)
    both = time_zh.total()
    tag[j] = (both[0] / lam_sum - both[1]) * control_buf[j]
    time_ag.start()

    @pl.when(early)
    def _():
        unit_rs.wait()
        uzh[dh] = unit_rs.total()
        unit_zh.start()

        time_ag.wait()
        for i in range(shards):
            left_buf[0:2 * groups, i * shard:(i + 1) * shard] = jnp.concatenate(
                halves(tag[i]), axis=0
            ).astype(bf16)
        left = left_buf[0:2 * groups, :]
        mid = units // 2
        acc = (dot_nn(left[:, :mid], high_buf[:mid, :]) + dot_nn(left[:, :mid], low_buf[:mid, :])) + (
            dot_nn(left[:, mid:], high_buf[mid:, :]) + dot_nn(left[:, mid:], low_buf[mid:, :])
        )
        grad[u] = acc[0:groups] + acc[groups:]
        time_grad.start()

    @pl.when(early)
    def _():
        unit_zh.wait()
        updated = raised_buf[j] / stat_buf[:, 0:1] * jnp.exp(-step_rate * unit_zh.total() / jnp.sqrt(before_len))
        uag[j] = updated
        utot[unit_tot.own] = to_row(jnp.sum(updated, axis=1, keepdims=True))
        unit_tot.start()
        unit_ag.start()

        time_grad.wait()
        ctrl_root = jnp.sqrt(jnp.maximum(stat_buf[:, 2:3], 1.0))
        moved = moved_buf[...] / lam_sum * jnp.exp(-step_rate * time_grad.total() / ctrl_root)
        moved_buf[...] = moved
        ttot[d] = to_row(jnp.sum(moved, axis=1, keepdims=True))
        time_tot.start()

        unit_tot.wait()
        uall[dc] = unit_tot.total() + to_row(stat_buf[:, 2:3], groups)
        unit_all.start()

    unit_ag.wait()
    unit_all.wait()
    unit_total = jnp.broadcast_to(to_col(unit_all.total(), groups), (groups, own_units))
    count = jnp.broadcast_to(to_col(uall[0], groups, groups), (groups, own_units))
    for i in range(early_ranks):
        unit_out[:, i * own_units:(i + 1) * own_units] = uag[i] / unit_total * count

    @pl.when(early)
    def _():
        time_tot.wait()
        time_out[...] = moved_buf[...] / to_col(time_tot.total(), groups) * before_len

    @pl.when(jnp.logical_not(early))
    def _():
        time_out[...] = jnp.zeros_like(time_out)

    for group in (time_rs, time_zh, lam_zh, time_ag):
        group.drain()

    @pl.when(early)
    def _():
        for group in (lam_rs, sum_x, sum_z, unit_rs, unit_zh, unit_tot, unit_ag, unit_all, time_grad, time_tot):
            group.drain()


def put_out(unit_in, time_in, unit_out, time_out, sems):
    copies = [
        pltpu.make_async_copy(unit_in, unit_out, sems.at[0]),
        pltpu.make_async_copy(time_in, time_out, sems.at[1]),
    ]
    for copy in copies:
        copy.start()
    for copy in copies:
        copy.wait()


def local(unit_split, day_split, outcomes, cohort, pre_end, post_start, unit_logit, time_logit):
    groups = pre_end.shape[0]
    units, days = outcomes.shape
    nx, nz = unit_split
    ny, nh, nc = day_split
    unit_n, day_n, shards = nx * nz, ny * nh * nc, ny * nc
    shard = units // shards
    own = shards // 2
    hbm = pl.BlockSpec(memory_space=pl.ANY)
    vmem = pl.BlockSpec(memory_space=pltpu.VMEM)
    dma = lambda n: pltpu.SemaphoreType.DMA((n,))
    slots = lambda n, size: pltpu.VMEM((n, groups, size), f32)
    rows = lambda n: pltpu.VMEM((n, 1, LANES), f32)
    unit_weights, time_weights = pl.pallas_call(
        functools.partial(kernel, unit_split, day_split),
        out_shape=(pltpu.VMEM((groups, units), f32), pltpu.VMEM((groups, days), f32)),
        in_specs=[hbm] * 6,
        out_specs=(vmem, vmem),
        scratch_shapes=[
            pltpu.SMEM((groups,), jnp.int32),
            pltpu.SMEM((groups,), jnp.int32),
            pltpu.VMEM((1, units), jnp.int32),
            pltpu.VMEM((groups, units), f32),
            pltpu.VMEM((groups, days), f32),
            pltpu.VMEM((units, days), f32),
            pltpu.VMEM((units, days), bf16),
            pltpu.VMEM((units, days), bf16),
            pltpu.VMEM((days, units), bf16),
            pltpu.VMEM((days, units), bf16),
            pltpu.VMEM((4 * groups, units), bf16),
            slots(own, units // own), slots(shards, shard),
            pltpu.VMEM((groups, days), f32),
            pltpu.VMEM((groups, LANES), f32),
            slots(nx, 2 * days + LANES), slots(nz, 2 * days + LANES), slots(unit_n, days),
            slots(own, units // own), slots(own, units // own), slots(nh, units // own), slots(shards, units // own),
            slots(shards, shard), slots(shards, shard),
            pltpu.VMEM((nh, 2, groups, shard), f32),
            slots(shards, shard),
            rows(shards), rows(nh), rows(unit_n * ny // 2), rows(2 * nc), rows(day_n // 2),
            dma(5),
            dma(PARTS),
            pltpu.SemaphoreType.REGULAR((2,)),
            *[dma(2)] * 14,
        ],
        compiler_params=pltpu.CompilerParams(collective_id=0, has_side_effects=True),
    )(pre_end, post_start, outcomes, cohort.reshape(1, units), unit_logit, time_logit)
    return pl.pallas_call(
        put_out,
        out_shape=(
            jax.ShapeDtypeStruct((groups, units), f32),
            jax.ShapeDtypeStruct((groups, days), f32),
        ),
        in_specs=[vmem] * 2,
        out_specs=(hbm, hbm),
        scratch_shapes=[dma(2)],
    )(*(pltpu.with_memory_space_constraint(v, pltpu.VMEM) for v in (unit_weights, time_weights)))


def solution(mesh):
    return jax.shard_map(
        functools.partial(local, UNIT_SPLIT, DAY_SPLIT),
        mesh=mesh,
        in_specs=(P("unit", "day"), P("unit"), P(), P(), P(None, "unit"), P(None, "day")),
        out_specs=(P(None, "unit"), P(None, "day")),
        check_vma=False,
    )
```
